32 devices in a mesh: dp: 8 (over y, x, core), ctx: 4 (over z).
Axes of the slice: x: 2, y: 2, z: 4, core: 2. Of those that a mesh axis runs over, the one named last changes fastest.
Arguments:
- layer_input: bfloat16 [8, 1024, 1024], P('dp', 'ctx'), may hold values from -6 to 6
- prefix: int32 [8], P('dp'), may hold values from 102 to 512, as said below
- ln1_gain: bfloat16 [1024], P(('dp', 'ctx')), may hold values from 0.5 to 1.5
- ln1_bias: bfloat16 [1024], P(('dp', 'ctx')), may hold values from -3 to 3
- w_qkv: bfloat16 [1024, 3072], P(('dp', 'ctx')), may hold values from -0.1875 to 0.1875
- b_qv: bfloat16 [2048], P(('dp', 'ctx')), may hold values from -4 to 4
- w_out: bfloat16 [1024, 1024], P(('dp', 'ctx')), may hold values from -3 to 3
- b_out: bfloat16 [1024], P(('dp', 'ctx')), may hold values from -3 to 3
- ln2_gain: bfloat16 [1024], P(('dp', 'ctx')), may hold values from 0.5 to 1.5
- ln2_bias: bfloat16 [1024], P(('dp', 'ctx')), may hold values from -3 to 3
- w_up: bfloat16 [1024, 4096], P(('dp', 'ctx')), may hold values from -0.1875 to 0.1875
- b_up: bfloat16 [4096], P(('dp', 'ctx')), may hold values from -4 to 4
- w_down: bfloat16 [4096, 1024], P(('dp', 'ctx')), may hold values from -0.09375 to 0.09375
- b_down: bfloat16 [1024], P(('dp', 'ctx')), may hold values from -6 to 6
- cotangent: bfloat16 [8, 1024, 1024], P('dp', 'ctx'), may hold values from -6 to 6
Outputs:
- layer_out: bfloat16 [8, 1024, 1024], P('dp', 'ctx')
- input_grad: float32 [8, 1024, 1024], P('dp', 'ctx')
- grad_ln1_gain: float32 [1024], P(('dp', 'ctx'))
- grad_ln1_bias: float32 [1024], P(('dp', 'ctx'))
- grad_w_qkv: float32 [1024, 3072], P(('dp', 'ctx'))
- grad_b_qv: float32 [2048], P(('dp', 'ctx'))
- grad_w_out: float32 [1024, 1024], P(('dp', 'ctx'))
- grad_b_out: float32 [1024], P(('dp', 'ctx'))
- grad_ln2_gain: float32 [1024], P(('dp', 'ctx'))
- grad_ln2_bias: float32 [1024], P(('dp', 'ctx'))
- grad_w_up: float32 [1024, 4096], P(('dp', 'ctx'))
- grad_b_up: float32 [4096], P(('dp', 'ctx'))
- grad_w_down: float32 [4096, 1024], P(('dp', 'ctx'))
- grad_b_down: float32 [1024], P(('dp', 'ctx'))
The draws below stay inside these ranges and needn't reach their ends.
Inputs may be any that keep to these rules, and one draw needn't show every extreme that they name: prefix[s] counts the leading positions of sequence s that attend to one another in both directions; the largest and the smallest allowed values both occur.
All inputs are finite; a program needn't handle non-finite values.
Results may differ from the reference program's by a relative error of at most 0.012.
Values may be sent and summed in bfloat16 or wider, within the bound.
No kernel may reach another device: no remote copies, remote signals or barrier semaphores. Data moves between devices by JAX's collectives and lax.ppermute only.
A program may use at most 192 MiB of HBM per device.

```python
import jax
import jax.numpy as jnp
from jax import lax

D = 1024
H = 16
HD = 64
FF = 4096
LEN = 1024
SEQS = 8


def draw_prefix(key, part):
    lowest = LEN // 10
    highest = LEN // 2
    drawn = jax.random.randint(jax.random.fold_in(key, 11), (SEQS,), lowest, highest + 1, dtype=jnp.int32)
    where_high = jax.random.randint(jax.random.fold_in(key, 12), (), 0, SEQS, dtype=jnp.int32)
    drawn = drawn.at[where_high].set(highest)
    return drawn.at[(where_high + 1) % SEQS].set(lowest)


def level_of(stream_key, dims, pieces, low, largest):
    def one(position, blocks):
        steps = jax.random.uniform(jax.random.fold_in(jax.random.fold_in(stream_key, 6), position), (blocks,), jnp.float32, low / len(pieces), largest / len(pieces))
        return jnp.repeat(jnp.exp(steps), dims[position] // blocks).reshape((-1,) + (1,) * (len(dims) - position - 1))

    loudness = one(*pieces[0])
    for cut in pieces[1:]:
        loudness = loudness * one(*cut)
    return loudness


def normal_values(own_key, shape, scale, reach, pieces=(), held_as=jnp.bfloat16):
    array = jax.random.normal(own_key, shape, jnp.float32) * scale
    if len(pieces) > 0:
        array = level_of(own_key, shape, pieces, -0.22, 0.18) * array
    return jnp.clip(array, min=-reach, max=reach).astype(held_as)


def setup_inputs(seed: int = 0) -> dict:
    keys = jax.random.split(jax.random.key(seed), 16)
    return {
        "layer_input": normal_values(keys[0], (SEQS, LEN, D), 1.0, 6.0, ((0, 8), (1, 4))),
        "prefix": draw_prefix(jax.random.fold_in(keys[15], 71), 0),
        "ln1_gain": jnp.clip(1.0 + 0.1 * jax.random.normal(keys[2], (D,), jnp.float32), 0.5, 1.5).astype(jnp.bfloat16),
        "ln1_bias": normal_values(keys[3], (D,), 0.2, 3.0, ((0, 32),)),
        "w_qkv": normal_values(keys[4], (D, 3 * D), D ** -0.5, 0.1875, ((0, 32),)),
        "b_qv": normal_values(keys[5], (2 * D,), 0.3, 4.0, ((0, 32),)),
        "w_out": normal_values(keys[6], (D, D), (D // 256) ** -0.5, 3.0, ((0, 32),)),
        "b_out": normal_values(keys[7], (D,), 0.2, 3.0, ((0, 32),)),
        "ln2_gain": jnp.clip(1.0 + 0.1 * jax.random.normal(keys[8], (D,), jnp.float32), 0.5, 1.5).astype(jnp.bfloat16),
        "ln2_bias": normal_values(keys[9], (D,), 0.2, 3.0, ((0, 32),)),
        "w_up": normal_values(keys[10], (D, FF), D ** -0.5, 0.1875, ((0, 32),)),
        "b_up": normal_values(keys[11], (FF,), 0.3, 4.0, ((0, 32),)),
        "w_down": normal_values(keys[12], (FF, D), FF ** -0.5, 0.09375, ((0, 32),)),
        "b_down": normal_values(keys[13], (D,), 0.4, 6.0, ((0, 32),)),
        "cotangent": normal_values(keys[14], (SEQS, LEN, D), 1.0, 6.0, ((0, 8), (1, 4))),
    }


HIGHEST = lax.Precision.HIGHEST
NEGATIVE = -1e+30

@jax.custom_vjp
def low(v):
    return lax.optimization_barrier(v.astype(jnp.bfloat16)).astype(jnp.float32)

@jax.custom_vjp
def low_back(v):
    return v

def low_keep(v):
    return (low(v), None)

def low_pass(kept, grad):
    return (grad,)

def back_keep(v):
    return (v, None)

def back_low(kept, grad):
    return (low(grad),)
low.defvjp(low_keep, low_pass)
low_back.defvjp(back_keep, back_low)

def layer_norm(values, gain, shift):
    center = lax.optimization_barrier(jnp.mean(values, axis=-1, keepdims=True))
    offsets = values - center
    spread = lax.optimization_barrier(jnp.mean(offsets * offsets, axis=-1, keepdims=True))
    return offsets * lax.rsqrt(spread + 1e-05) * gain + shift

def gelu_tanh(values):
    return jax.nn.gelu(values, approximate=True)

def attend_rows(query_rows, row_start, key_heads, value_heads, prefix_len):
    row_count = query_rows.shape[0]
    raw_scores = low_back(jnp.einsum('qhd,khd->hqk', query_rows, key_heads, precision=HIGHEST) * 0.125)
    query_pos = row_start + jnp.arange(row_count, dtype=jnp.int32)
    key_pos = jnp.arange(key_heads.shape[0], dtype=jnp.int32)
    allowed = (key_pos[None, :] <= query_pos[:, None]) | (key_pos[None, :] < prefix_len)
    masked = jnp.where(allowed[None], raw_scores, NEGATIVE)
    row_max = lax.optimization_barrier(jnp.max(masked, axis=-1, keepdims=True))
    log_total = row_max + jnp.log(lax.optimization_barrier(jnp.sum(jnp.exp(masked - row_max), axis=-1, keepdims=True)))
    weights_soft = low(jnp.exp(masked - log_total))
    return jnp.einsum('hqk,khd->qhd', weights_soft, value_heads, precision=HIGHEST)

def forward(params, inputs, prefix_len):
    gain_first, shift_first, proj_qkv, bias_qv, proj_out, bias_out, gain_second, shift_second, proj_up, bias_up, proj_down, bias_down = params
    length = inputs.shape[0]
    hidden_first = low(layer_norm(inputs, gain_first, shift_first))
    mixed = jnp.dot(hidden_first, proj_qkv, precision=HIGHEST)
    queries = low_back(low(mixed[:, :D] + bias_qv[:D])).reshape(length, H, HD)
    key_heads = low_back(low(mixed[:, D:2 * D])).reshape(length, H, HD)
    value_heads = low_back(low(mixed[:, 2 * D:] + bias_qv[D:])).reshape(length, H, HD)
    block_rows = min(512, length)
    block_count = length // block_rows
    query_blocks = queries.reshape(block_count, block_rows, H, HD)
    block_starts = jnp.arange(block_count, dtype=jnp.int32) * block_rows
    saved_attend = jax.checkpoint(attend_rows)

    def one_block(element):
        return saved_attend(element[0], element[1], key_heads, value_heads, prefix_len)
    attended = lax.map(one_block, (query_blocks, block_starts))
    attended = low_back(low(attended.reshape(length, D)))
    branch_one = low_back(jnp.dot(attended, proj_out, precision=HIGHEST) + bias_out)
    resid = inputs + branch_one
    hidden_second = low(layer_norm(resid, gain_second, shift_second))
    pre_act = low_back(jnp.dot(hidden_second, proj_up, precision=HIGHEST) + bias_up)
    activ = low(gelu_tanh(pre_act))
    branch_two = low_back(jnp.dot(activ, proj_down, precision=HIGHEST) + bias_down)
    return resid + branch_two

def reference(layer_input, prefix, ln1_gain, ln1_bias, w_qkv, b_qv, w_out, b_out, ln2_gain, ln2_bias, w_up, b_up, w_down, b_down, cotangent):
    params = tuple((tensor.astype(jnp.float32) for tensor in (ln1_gain, ln1_bias, w_qkv, b_qv, w_out, b_out, ln2_gain, ln2_bias, w_up, b_up, w_down, b_down)))

    def per_sequence(sums, element):
        inputs, grad_output, prefix_len = element
        output, pullback = jax.vjp(lambda weights, values: forward(weights, values, prefix_len), params, inputs.astype(jnp.float32))
        param_grads, input_grads = pullback(grad_output.astype(jnp.float32))
        sums = tuple((earlier + latest for earlier, latest in zip(sums, param_grads)))
        return (sums, (output.astype(jnp.bfloat16), input_grads))
    zeros_init = tuple((jnp.zeros(tensor.shape, jnp.float32) for tensor in params))
    sums, (outputs, input_grads) = lax.scan(per_sequence, zeros_init, (layer_input, cotangent, prefix))
    return (outputs, input_grads, sums[0], sums[1], sums[2], sums[3], sums[4], sums[5], sums[6], sums[7], sums[8], sums[9], sums[10], sums[11])
```

```python
import functools

import jax
import jax.numpy as jnp
from jax import lax
from jax.experimental import pallas as pl
from jax.experimental.pallas import tpu as pltpu
from jax.sharding import PartitionSpec as P

HEADS = 16
HD = 64
SCALE = 0.125
NEGATIVE = -1e30
AXES = ("dp", "ctx")
F32 = jnp.float32
BF16 = jnp.bfloat16


def dot_nt(a, b):
    return lax.dot_general(a, b, (((1,), (1,)), ((), ())), preferred_element_type=F32)


def dot_tn(a, b):
    return lax.dot_general(a, b, (((0,), (0,)), ((), ())), preferred_element_type=F32)


def dot_nn(a, b):
    return lax.dot_general(a, b, (((1,), (0,)), ((), ())), preferred_element_type=F32)


def allowed_keys(limit, rows, first_query, prefix_len):
    key_pos = lax.broadcasted_iota(jnp.int32, (limit, rows), 0)
    query_pos = lax.broadcasted_iota(jnp.int32, (limit, rows), 1) + first_query
    return (key_pos <= query_pos) | (key_pos < prefix_len)


def over_blocks(length, rows, step):
    if length <= 1024:
        for first in range(0, length, rows):
            step(first, max(length // 2, first + rows))
    else:

        def body(i, carry):
            step(pl.multiple_of(i * rows, rows), length)
            return carry

        lax.fori_loop(0, length // rows, body, 0)


def attend_forward(prefix_ref, q_ref, k_ref, v_ref, o_ref, lse_ref, *, rows):
    length, width = q_ref.shape
    group = width // HD
    prefix_len = prefix_ref[0]
    lane_head = lax.broadcasted_iota(jnp.int32, (1, width), 1) // HD

    def step(first, limit):
        block = pl.ds(first, rows)
        queries = q_ref[block, :] * SCALE
        keys = k_ref[:limit, :]
        values = v_ref[:limit, :]
        allowed = allowed_keys(limit, rows, first, prefix_len)
        attended = jnp.zeros((rows, width), F32)
        for h in range(group):
            mine = lane_head == h
            scores = dot_nt(keys, jnp.where(mine, queries, 0).astype(BF16))
            scores = jnp.where(allowed, scores, NEGATIVE)
            top = jnp.max(scores, axis=0, keepdims=True)
            terms = jnp.exp(scores - top)
            total = jnp.sum(terms, axis=0, keepdims=True)
            lse_ref[h, :, block] = top + jnp.log(total)
            weights = (terms * (1.0 / total)).astype(BF16)
            attended = jnp.where(mine, dot_tn(weights, values), attended)
        o_ref[block, :] = attended.astype(BF16)

    over_blocks(length, rows, step)


def attend_backward(
    prefix_ref, q_ref, k_ref, v_ref, o_ref, do_ref, lse_ref, dq_ref, dk_ref, dv_ref, dk_sum, dv_sum, *, rows
):
    length, width = q_ref.shape
    group = width // HD
    prefix_len = prefix_ref[0]
    lane_head = lax.broadcasted_iota(jnp.int32, (1, width), 1) // HD
    dk_sum[...] = jnp.zeros_like(dk_sum)
    dv_sum[...] = jnp.zeros_like(dv_sum)

    def step(first, limit):
        block = pl.ds(first, rows)
        queries = q_ref[block, :] * SCALE
        grads = do_ref[block, :]
        keys = k_ref[:limit, :]
        values = v_ref[:limit, :]
        allowed = allowed_keys(limit, rows, first, prefix_len)
        products = (grads.astype(F32) * o_ref[block, :].astype(F32)).T
        query_grad = jnp.zeros((rows, width), F32)
        for h in range(group):
            mine = lane_head == h
            queries_h = jnp.where(mine, queries, 0).astype(BF16)
            grads_h = jnp.where(mine, grads, 0).astype(BF16)
            delta = jnp.sum(products[h * HD : (h + 1) * HD, :], axis=0, keepdims=True)
            scores = jnp.where(allowed, dot_nt(keys, queries_h), NEGATIVE)
            probs = jnp.exp(scores - lse_ref[h, :, block])
            weight_grad = dot_nt(values, grads_h)
            score_grad = (probs * (weight_grad - delta)).astype(BF16)
            dv_sum[:limit, :] += dot_nn(probs.astype(BF16), grads_h)
            dk_sum[:limit, :] += dot_nn(score_grad, queries_h)
            query_grad = jnp.where(mine, dot_tn(score_grad, keys), query_grad)
        dq_ref[block, :] = (query_grad * SCALE).astype(BF16)

    over_blocks(length, rows, step)
    dk_ref[...] = dk_sum[...].astype(BF16)
    dv_ref[...] = dv_sum[...].astype(BF16)


def attention_shapes(mixed):
    length, width = mixed.shape
    heads = width // (3 * HD)
    group = 2 if heads % 2 == 0 else 1
    return length, heads, group, heads // group, group * HD


def thirds(mixed, count, lanes):
    length, width = mixed.shape
    part = lambda n: pl.BlockSpec((length, lanes), lambda g: (0, n * count + g))
    if lanes % 128 == 0:
        return [mixed] * 3, [part(0), part(1), part(2)]
    return [mixed[:, n * width // 3 : (n + 1) * width // 3] for n in range(3)], [part(0)] * 3


def attention(prefix, mixed):
    length, heads, group, count, lanes = attention_shapes(mixed)
    operands, columns = thirds(mixed, count, lanes)
    return pl.pallas_call(
        functools.partial(attend_forward, rows=min(256, length)),
        grid=(count,),
        in_specs=[pl.BlockSpec(memory_space=pltpu.SMEM)] + columns,
        out_specs=[
            pl.BlockSpec((length, lanes), lambda g: (0, g)),
            pl.BlockSpec((group, 1, length), lambda g: (g, 0, 0)),
        ],
        out_shape=[
            jax.ShapeDtypeStruct((length, heads * HD), BF16),
            jax.ShapeDtypeStruct((heads, 1, length), F32),
        ],
        compiler_params=pltpu.CompilerParams(vmem_limit_bytes=48 * 2**20),
        name="attend_forward",
    )(prefix, *operands)


def attention_grads(prefix, mixed, attended, grad_attended, log_total):
    length, heads, group, count, lanes = attention_shapes(mixed)
    operands, columns = thirds(mixed, count, lanes)
    own = pl.BlockSpec((length, lanes), lambda g: (0, g))
    wide = jax.ShapeDtypeStruct((length, heads * HD), BF16)
    return pl.pallas_call(
        functools.partial(attend_backward, rows=min(256, length)),
        grid=(count,),
        in_specs=[
            pl.BlockSpec(memory_space=pltpu.SMEM),
            *columns,
            own,
            own,
            pl.BlockSpec((group, 1, length), lambda g: (g, 0, 0)),
        ],
        out_specs=[own] * 3,
        out_shape=[wide] * 3,
        scratch_shapes=[pltpu.VMEM((length, lanes), F32)] * 2,
        compiler_params=pltpu.CompilerParams(vmem_limit_bytes=48 * 2**20),
        name="attend_backward",
    )(prefix, *operands, attended, grad_attended, log_total)


def bits_of(size):
    return size.bit_length() - 1


def rank(bit):
    return (0 if bit[0] == "ctx" else 1, bit[1])


def my_bit(bit):
    return (lax.axis_index(bit[0]) >> bit[1]) & 1


def swap_by(x, dp_mask, ctx_mask):
    dp, ctx = lax.axis_size("dp"), lax.axis_size("ctx")
    pairs = [
        (d * ctx + c, (d ^ dp_mask) * ctx + (c ^ ctx_mask)) for d in range(dp) for c in range(ctx)
    ]
    return lax.ppermute(x, AXES, pairs)


def swap(x, bit):
    return swap_by(x, 1 << bit[1], 0) if bit[0] == "dp" else swap_by(x, 0, 1 << bit[1])


def join(own, other, here, axis):
    first = here == 0
    return jnp.stack([jnp.where(first, own, other), jnp.where(first, other, own)], axis)


def gather(x, bits, done=()):
    done = list(done)
    for bit in bits:
        place = sum(rank(d) > rank(bit) for d in done)
        x = join(x, swap(x, bit), my_bit(bit), place)
        done.append(bit)
    return x


def scatter(x, bits, left=()):
    remaining = sorted(list(bits) + list(left), key=rank, reverse=True)
    for n, bit in enumerate(bits):
        place = remaining.index(bit)
        here = my_bit(bit)
        sent = lax.dynamic_index_in_dim(x, 1 - here, place, keepdims=False)
        kept = lax.dynamic_index_in_dim(x, here, place, keepdims=False)
        x = kept.astype(F32) + swap(sent, bit).astype(F32)
        remaining.pop(place)
        if n + 1 < len(bits):
            x = x.astype(sent.dtype)
    return x


def unrelate(pieces):
    me = lax.axis_index("ctx")
    for b in range(bits_of(len(pieces))):
        flip = ((me >> b) & 1) == 1
        pieces = [jnp.where(flip, pieces[j ^ (1 << b)], pieces[j]) for j in range(len(pieces))]
    return pieces


def gather_ctx(x):
    return unrelate([x] + [swap_by(x, 0, s) for s in range(1, lax.axis_size("ctx"))])


def exchange_ctx(x):
    me = lax.axis_index("ctx")
    pick = lambda j: lax.dynamic_index_in_dim(x, j, 0, keepdims=False)
    return unrelate(
        [pick(me)] + [swap_by(pick(me ^ s), 0, s) for s in range(1, lax.axis_size("ctx"))]
    )


def sum_ctx(x):
    me = lax.axis_index("ctx")
    pick = lambda j: lax.dynamic_index_in_dim(x, j, 0, keepdims=False)
    total = pick(me).astype(F32)
    for s in range(1, lax.axis_size("ctx")):
        total = total + swap_by(pick(me ^ s).astype(BF16), 0, s).astype(F32)
    return total


def normalize(values):
    center = jnp.mean(values, axis=-1, keepdims=True)
    offsets = values - center
    spread = jnp.mean(offsets * offsets, axis=-1, keepdims=True)
    scale = lax.rsqrt(spread + 1e-05)
    return offsets * scale, scale


def norm_back(grad, gain, hat, scale):
    e = grad * gain
    return scale * (
        e
        - jnp.mean(e, axis=-1, keepdims=True)
        - hat * jnp.mean(e * hat, axis=-1, keepdims=True)
    )


def gelu_tanh(values):
    return jax.nn.gelu(values, approximate=True)


def per_device(
    layer_input,
    prefix,
    ln1_gain,
    ln1_bias,
    w_qkv,
    b_qv,
    w_out,
    b_out,
    ln2_gain,
    ln2_bias,
    w_up,
    b_up,
    w_down,
    b_down,
    cotangent,
):
    dp, ctx = lax.axis_size("dp"), lax.axis_size("ctx")
    devices = dp * ctx
    planes = dp // 2
    tokens, d = layer_input.shape[1:]
    length = tokens * ctx
    width = HEADS * HD // ctx
    ff = b_up.shape[0] * devices
    chunk = ff // 4
    piece = b_up.shape[0] // 2
    rows = d // devices
    core_bit = ("dp", 0)
    plane_bits = [("dp", b) for b in range(1, bits_of(dp))]
    ctx_bits = [("ctx", b) for b in range(bits_of(ctx))]
    twos = lambda bits: (2,) * len(bits)
    core = my_bit(core_bit)
    z = lax.axis_index("ctx")
    x_own = layer_input[0]
    cot_own = cotangent[0]

    small = [ln1_gain, ln1_bias, b_qv, b_out, ln2_gain, ln2_bias, b_up, b_down]
    sizes = [s.shape[0] for s in small]
    packed = gather(jnp.concatenate(small)[None], ctx_bits + [core_bit] + plane_bits)
    packed = packed.reshape(devices, sum(sizes))
    whole = []
    start = 0
    for size in sizes:
        whole.append(packed[:, start : start + size].reshape(devices * size).astype(F32))
        start += size
    gain_first, shift_first, bias_qv, bias_out, gain_second, shift_second, bias_up, bias_down = whole

    by_head = w_qkv.reshape(rows, 3, ctx, width).transpose(2, 0, 1, 3).reshape(ctx, rows, 3 * width)
    own_cols = jnp.stack(exchange_ctx(by_head), 0)
    proj_qkv = gather(own_cols, plane_bits + [core_bit]).reshape(d, 3 * width)

    inputs_all = jnp.concatenate(gather_ctx(x_own), 0)

    up_cols = w_up.reshape(rows, planes, 2, ctx, 2, piece)
    up_pair = join(
        lax.dynamic_index_in_dim(up_cols, core, 2, keepdims=False),
        swap(lax.dynamic_index_in_dim(up_cols, 1 - core, 2, keepdims=False), core_bit),
        core,
        0,
    )
    orders = (plane_bits, plane_bits[::-1])
    proj_up, proj_down, bias_ups = [], [], []
    bias_up_core = lax.dynamic_index_in_dim(
        bias_up.reshape(planes, 2, ctx, 2, piece), core, 1, keepdims=False
    )
    for c in range(2):
        part = up_pair[:, :, :, :, c].reshape(2, rows, planes * ctx * piece)
        proj_up.append(gather(part, ctx_bits + orders[c], [core_bit]).reshape(d, chunk))
        part = w_down[c * piece : (c + 1) * piece]
        proj_down.append(gather(part, ctx_bits + orders[c]).reshape(chunk, d))
        bias_ups.append(bias_up_core[:, :, c].reshape(chunk))
    proj_out = gather(w_out, ctx_bits + plane_bits[::-1] + [core_bit]).reshape(d, d)

    hat_all, scale_all = normalize(inputs_all.astype(F32))
    hidden_first = (hat_all * gain_first + shift_first).astype(BF16)
    mixed = jnp.dot(hidden_first, proj_qkv, preferred_element_type=F32)
    bias_heads = lax.dynamic_index_in_dim(bias_qv.reshape(2, ctx, width), z, 1, keepdims=False)
    bias_mixed = jnp.concatenate([bias_heads[0], jnp.zeros((width,), F32), bias_heads[1]])
    mixed = (mixed + bias_mixed).astype(BF16)
    attended_heads, log_total = attention(prefix, mixed)
    attended = jnp.concatenate(exchange_ctx(attended_heads.reshape(ctx, tokens, width)), 1)

    inputs = x_own.astype(F32)
    resid = inputs + jnp.dot(attended, proj_out, preferred_element_type=F32) + bias_out
    hat_second, scale_second = normalize(resid)
    hidden_second = (hat_second * gain_second + shift_second).astype(BF16)

    pair = lambda t: jnp.concatenate([t, swap(t, core_bit)], 0)
    hidden_pair = pair(hidden_second)
    cot_pair = pair(cot_own)
    split_sum = lambda t: t[:tokens] + swap(t[tokens:].astype(BF16), core_bit).astype(F32)
    out_part = 0.0
    grad_hidden_part = 0.0
    grads_down, grads_up, grads_bias_up = [], [], []
    for c in range(2):
        pre_act = (
            jnp.dot(hidden_pair, proj_up[c], preferred_element_type=F32) + bias_ups[c]
        )
        gelu_value, gelu_pull = jax.vjp(gelu_tanh, pre_act)
        activ = gelu_value.astype(BF16)
        out_part += jnp.dot(activ, proj_down[c], preferred_element_type=F32)
        grad_activ = dot_nt(cot_pair, proj_down[c])
        grad_pre = gelu_pull(grad_activ)[0].astype(BF16)
        grads_bias_up.append(jnp.sum(grad_pre.astype(F32), axis=0))
        grad_hidden_part += dot_nt(grad_pre, proj_up[c])
        grad = dot_tn(activ, cot_pair).astype(BF16)
        grad = grad.reshape(twos(plane_bits) + twos(ctx_bits) + (piece, d))
        grads_down.append(scatter(grad, orders[c] + ctx_bits[::-1]))
        grad = dot_tn(hidden_pair, grad_pre).astype(BF16)
        grad = grad.reshape(twos(plane_bits) + (2,) + twos(ctx_bits) + (rows, chunk))
        grads_up.append(scatter(grad, orders[c] + ctx_bits[::-1], [core_bit]))
    layer_out = (resid + split_sum(out_part) + bias_down).astype(BF16)
    sum_down = jnp.concatenate(grads_down, 0)
    up_sum = jnp.stack([g.reshape(2, rows, planes, ctx, piece) for g in grads_up], 4)
    sum_up = join(
        lax.dynamic_index_in_dim(up_sum, core, 0, keepdims=False),
        swap(lax.dynamic_index_in_dim(up_sum, 1 - core, 0, keepdims=False).astype(BF16), core_bit).astype(F32),
        core,
        2,
    ).reshape(rows, ff)

    grad_hidden_second = split_sum(grad_hidden_part)
    upstream = cot_own.astype(F32)
    grad_gain_second = jnp.sum(grad_hidden_second * hat_second, axis=0)
    grad_shift_second = jnp.sum(grad_hidden_second, axis=0)
    grad_resid = upstream + norm_back(grad_hidden_second, gain_second, hat_second, scale_second)
    grad_branch = grad_resid.astype(BF16)
    grad_bias_out = jnp.sum(grad_branch.astype(F32), axis=0)
    grad_attended = dot_nt(grad_branch, proj_out).astype(BF16)
    grad_heads = jnp.concatenate(
        exchange_ctx(grad_attended.reshape(tokens, ctx, width).transpose(1, 0, 2)), 0
    )
    grad_out = dot_tn(attended, grad_branch).astype(BF16)
    grad_out = grad_out.reshape(twos(plane_bits) + (2,) + twos(ctx_bits) + (rows, d))
    sum_out = scatter(grad_out, [core_bit] + plane_bits + ctx_bits[::-1])

    grad_q, grad_k, grad_v = attention_grads(prefix, mixed, attended_heads, grad_heads, log_total)
    grad_mixed = jnp.concatenate([grad_q, grad_k, grad_v], 1)
    grad_hidden_all = dot_nt(grad_mixed, proj_qkv)
    grad_qkv = dot_tn(hidden_first, grad_mixed).astype(BF16)
    grad_qkv = grad_qkv.reshape((2,) * bits_of(dp) + (ctx * rows, 3 * width))
    own_rows = scatter(grad_qkv, [core_bit] + plane_bits).astype(BF16)
    columns = exchange_ctx(own_rows.reshape(ctx, rows, 3 * width))
    sum_qkv = (
        jnp.stack([c.reshape(rows, 3, width) for c in columns], 2)
        .reshape(rows, 3 * d)
        .astype(F32)
    )

    grad_gain_first = jnp.sum(grad_hidden_all * hat_all, axis=0)
    grad_shift_first = jnp.sum(grad_hidden_all, axis=0)
    grad_hidden_first = sum_ctx(grad_hidden_all.reshape(ctx, tokens, d))
    hat_first, scale_first = normalize(inputs)
    input_grad = grad_resid + norm_back(grad_hidden_first, gain_first, hat_first, scale_first)

    sums_heads = jnp.sum(grad_mixed.astype(F32), axis=0).reshape(3, 1, width)
    at_heads = lambda t: lax.dynamic_update_slice(jnp.zeros((1, ctx, width), F32), t[None], (0, z, 0))
    grad_bias_qv = jnp.concatenate([at_heads(sums_heads[0]), at_heads(sums_heads[2])], 0)
    up_own = jnp.stack([g.reshape(planes, 1, ctx, piece) for g in grads_bias_up], 3)
    grad_bias_up = lax.dynamic_update_slice(
        jnp.zeros((planes, 2, ctx, 2, piece), F32), up_own, (0, core, 0, 0, 0)
    )
    grad_bias_down = jnp.sum(upstream, axis=0)
    grads = [
        grad_gain_first,
        grad_shift_first,
        grad_bias_qv,
        grad_bias_out,
        grad_gain_second,
        grad_shift_second,
        grad_bias_up,
        grad_bias_down,
    ]
    packed = jnp.concatenate([g.reshape(devices, size) for g, size in zip(grads, sizes)], 1)
    packed = packed.reshape((2,) * bits_of(devices) + (1, sum(sizes)))
    packed = scatter(packed, plane_bits + [core_bit] + ctx_bits)[0]
    sums = []
    start = 0
    for size in sizes:
        sums.append(packed[start : start + size])
        start += size
    (
        sum_gain_first,
        sum_shift_first,
        sum_bias_qv,
        sum_bias_out,
        sum_gain_second,
        sum_shift_second,
        sum_bias_up,
        sum_bias_down,
    ) = sums
    return (
        layer_out[None],
        input_grad[None],
        sum_gain_first,
        sum_shift_first,
        sum_qkv,
        sum_bias_qv,
        sum_out,
        sum_bias_out,
        sum_gain_second,
        sum_shift_second,
        sum_up,
        sum_bias_up,
        sum_down,
        sum_bias_down,
    )


def solution(mesh):
    vector = P(AXES)
    matrix = P(AXES, None)
    tokens = P("dp", "ctx", None)
    return jax.shard_map(
        per_device,
        mesh=mesh,
        in_specs=(
            tokens,
            P("dp"),
            vector,
            vector,
            matrix,
            vector,
            matrix,
            vector,
            vector,
            vector,
            matrix,
            vector,
            matrix,
            vector,
            tokens,
        ),
        out_specs=(
            tokens,
            tokens,
            vector,
            vector,
            matrix,
            vector,
            matrix,
            vector,
            vector,
            vector,
            matrix,
            vector,
            matrix,
            vector,
        ),
        check_vma=False,
    )
```

```python
import functools

import jax
import jax.numpy as jnp
from jax import lax
from jax.experimental import pallas as pl
from jax.experimental.pallas import tpu as pltpu
from jax.sharding import PartitionSpec as P

HEADS = 16
HD = 64
SCALE = 0.125
NEGATIVE = -1e30
AXES = ("dp", "ctx")
F32 = jnp.float32
BF16 = jnp.bfloat16


def dot_nt(a, b):
    return lax.dot_general(a, b, (((1,), (1,)), ((), ())), preferred_element_type=F32)


def dot_tn(a, b):
    return lax.dot_general(a, b, (((0,), (0,)), ((), ())), preferred_element_type=F32)


def dot_nn(a, b):
    return lax.dot_general(a, b, (((1,), (0,)), ((), ())), preferred_element_type=F32)


def allowed_keys(limit, rows, first_query, prefix_len):
    key_pos = lax.broadcasted_iota(jnp.int32, (limit, rows), 0)
    query_pos = lax.broadcasted_iota(jnp.int32, (limit, rows), 1) + first_query
    return (key_pos <= query_pos) | (key_pos < prefix_len)


def over_blocks(length, rows, step):
    if length <= 1024:
        for first in range(0, length, rows):
            step(first, max(length // 2, first + rows))
    else:

        def body(i, carry):
            step(pl.multiple_of(i * rows, rows), length)
            return carry

        lax.fori_loop(0, length // rows, body, 0)


def attend_forward(prefix_ref, q_ref, k_ref, v_ref, o_ref, lse_ref, *, rows):
    length, width = q_ref.shape
    group = width // HD
    prefix_len = prefix_ref[0]
    lane_head = lax.broadcasted_iota(jnp.int32, (1, width), 1) // HD

    def step(first, limit):
        block = pl.ds(first, rows)
        queries = q_ref[block, :] * SCALE
        keys = k_ref[:limit, :]
        values = v_ref[:limit, :]
        allowed = allowed_keys(limit, rows, first, prefix_len)
        attended = jnp.zeros((rows, width), F32)
        for h in range(group):
            mine = lane_head == h
            scores = dot_nt(keys, jnp.where(mine, queries, 0).astype(BF16))
            scores = jnp.where(allowed, scores, NEGATIVE)
            top = jnp.max(scores, axis=0, keepdims=True)
            terms = jnp.exp(scores - top)
            total = jnp.sum(terms, axis=0, keepdims=True)
            lse_ref[h, :, block] = top + jnp.log(total)
            weights = (terms * (1.0 / total)).astype(BF16)
            attended = jnp.where(mine, dot_tn(weights, values), attended)
        o_ref[block, :] = attended.astype(BF16)

    over_blocks(length, rows, step)


def attend_backward(
    prefix_ref, q_ref, k_ref, v_ref, o_ref, do_ref, lse_ref, dq_ref, dk_ref, dv_ref, dk_sum, dv_sum, *, rows
):
    length, width = q_ref.shape
    group = width // HD
    prefix_len = prefix_ref[0]
    lane_head = lax.broadcasted_iota(jnp.int32, (1, width), 1) // HD
    dk_sum[...] = jnp.zeros_like(dk_sum)
    dv_sum[...] = jnp.zeros_like(dv_sum)

    def step(first, limit):
        block = pl.ds(first, rows)
        queries = q_ref[block, :] * SCALE
        grads = do_ref[block, :]
        keys = k_ref[:limit, :]
        values = v_ref[:limit, :]
        allowed = allowed_keys(limit, rows, first, prefix_len)
        products = (grads.astype(F32) * o_ref[block, :].astype(F32)).T
        query_grad = jnp.zeros((rows, width), F32)
        for h in range(group):
            mine = lane_head == h
            queries_h = jnp.where(mine, queries, 0).astype(BF16)
            grads_h = jnp.where(mine, grads, 0).astype(BF16)
            delta = jnp.sum(products[h * HD : (h + 1) * HD, :], axis=0, keepdims=True)
            scores = jnp.where(allowed, dot_nt(keys, queries_h), NEGATIVE)
            probs = jnp.exp(scores - lse_ref[h, :, block])
            weight_grad = dot_nt(values, grads_h)
            score_grad = (probs * (weight_grad - delta)).astype(BF16)
            dv_sum[:limit, :] += dot_nn(probs.astype(BF16), grads_h)
            dk_sum[:limit, :] += dot_nn(score_grad, queries_h)
            query_grad = jnp.where(mine, dot_tn(score_grad, keys), query_grad)
        dq_ref[block, :] = (query_grad * SCALE).astype(BF16)

    over_blocks(length, rows, step)
    dk_ref[...] = dk_sum[...].astype(BF16)
    dv_ref[...] = dv_sum[...].astype(BF16)


def attention_shapes(mixed):
    length, width = mixed.shape
    heads = width // (3 * HD)
    group = 2 if heads % 2 == 0 else 1
    return length, heads, group, heads // group, group * HD


def thirds(mixed, count, lanes):
    length, width = mixed.shape
    part = lambda n: pl.BlockSpec((length, lanes), lambda g: (0, n * count + g))
    if lanes % 128 == 0:
        return [mixed] * 3, [part(0), part(1), part(2)]
    return [mixed[:, n * width // 3 : (n + 1) * width // 3] for n in range(3)], [part(0)] * 3


def attention(prefix, mixed):
    length, heads, group, count, lanes = attention_shapes(mixed)
    operands, columns = thirds(mixed, count, lanes)
    return pl.pallas_call(
        functools.partial(attend_forward, rows=min(256, length)),
        grid=(count,),
        in_specs=[pl.BlockSpec(memory_space=pltpu.SMEM)] + columns,
        out_specs=[
            pl.BlockSpec((length, lanes), lambda g: (0, g)),
            pl.BlockSpec((group, 1, length), lambda g: (g, 0, 0)),
        ],
        out_shape=[
            jax.ShapeDtypeStruct((length, heads * HD), BF16),
            jax.ShapeDtypeStruct((heads, 1, length), F32),
        ],
        compiler_params=pltpu.CompilerParams(vmem_limit_bytes=48 * 2**20),
        name="attend_forward",
    )(prefix, *operands)


def attention_grads(prefix, mixed, attended, grad_attended, log_total):
    length, heads, group, count, lanes = attention_shapes(mixed)
    operands, columns = thirds(mixed, count, lanes)
    own = pl.BlockSpec((length, lanes), lambda g: (0, g))
    wide = jax.ShapeDtypeStruct((length, heads * HD), BF16)
    return pl.pallas_call(
        functools.partial(attend_backward, rows=min(256, length)),
        grid=(count,),
        in_specs=[
            pl.BlockSpec(memory_space=pltpu.SMEM),
            *columns,
            own,
            own,
            pl.BlockSpec((group, 1, length), lambda g: (g, 0, 0)),
        ],
        out_specs=[own] * 3,
        out_shape=[wide] * 3,
        scratch_shapes=[pltpu.VMEM((length, lanes), F32)] * 2,
        compiler_params=pltpu.CompilerParams(vmem_limit_bytes=48 * 2**20),
        name="attend_backward",
    )(prefix, *operands, attended, grad_attended, log_total)


def bits_of(size):
    return size.bit_length() - 1


def rank(bit):
    return (0 if bit[0] == "ctx" else 1, bit[1])


def my_bit(bit):
    return (lax.axis_index(bit[0]) >> bit[1]) & 1


def swap_by(x, dp_mask, ctx_mask):
    dp, ctx = lax.axis_size("dp"), lax.axis_size("ctx")
    pairs = [
        (d * ctx + c, (d ^ dp_mask) * ctx + (c ^ ctx_mask)) for d in range(dp) for c in range(ctx)
    ]
    return lax.ppermute(x, AXES, pairs)


def swap(x, bit):
    return swap_by(x, 1 << bit[1], 0) if bit[0] == "dp" else swap_by(x, 0, 1 << bit[1])


def join(own, other, here, axis):
    first = here == 0
    return jnp.stack([jnp.where(first, own, other), jnp.where(first, other, own)], axis)


def gather(x, bits, done=()):
    done = list(done)
    for bit in bits:
        place = sum(rank(d) > rank(bit) for d in done)
        x = join(x, swap(x, bit), my_bit(bit), place)
        done.append(bit)
    return x


def scatter(x, bits, left=(), last=F32):
    remaining = sorted(list(bits) + list(left), key=rank, reverse=True)
    for n, bit in enumerate(bits):
        place = remaining.index(bit)
        here = my_bit(bit)
        sent = lax.dynamic_index_in_dim(x, 1 - here, place, keepdims=False)
        kept = lax.dynamic_index_in_dim(x, here, place, keepdims=False)
        x = kept.astype(F32) + swap(sent, bit).astype(F32)
        remaining.pop(place)
        x = x.astype(sent.dtype if n + 1 < len(bits) else last)
    return x


def unrelate(pieces, me):
    for b in range(bits_of(len(pieces))):
        flip = ((me >> b) & 1) == 1
        pieces = [jnp.where(flip, pieces[j ^ (1 << b)], pieces[j]) for j in range(len(pieces))]
    return pieces


def gather_ctx(x):
    others = [swap_by(x, 0, s) for s in range(1, lax.axis_size("ctx"))]
    return unrelate([x] + others, lax.axis_index("ctx"))


def exchange_ctx(pick):
    me = lax.axis_index("ctx")
    others = [swap_by(pick(me ^ s), 0, s) for s in range(1, lax.axis_size("ctx"))]
    return unrelate([pick(me)] + others, me)


def exchange_planes(pick):
    me = lax.axis_index("dp") >> 1
    others = [swap_by(pick(me ^ s), s << 1, 0) for s in range(1, lax.axis_size("dp") // 2)]
    return unrelate([pick(me)] + others, me)


def pool_rows(x, orders):
    count = x.shape[0] // 2
    halves = []
    for part, bits in zip((x[:count], x[count:]), orders):
        part = part[None]
        for bit in bits:
            part = jnp.concatenate([part, swap(part, bit)], 0)
        halves.append(part)
    return jnp.concatenate(halves, 0).reshape(-1, x.shape[1])


def share_rows(x, orders):
    planes = 2 ** len(orders[0])
    x = x.reshape(2, planes, x.shape[0] // (2 * planes), x.shape[1])
    halves = []
    for part, bits in zip((x[0], x[1]), orders):
        for bit in reversed(bits):
            count = part.shape[0] // 2
            other = swap(part[count:].astype(BF16), bit)
            part = part[:count].astype(F32) + other.astype(F32)
        halves.append(part[0])
    return jnp.concatenate(halves, 0)


def sum_ctx(pick):
    me = lax.axis_index("ctx")
    total = pick(me).astype(F32)
    for s in range(1, lax.axis_size("ctx")):
        total = total + swap_by(pick(me ^ s), 0, s).astype(F32)
    return total


def send_ctx(x, steps):
    ctx = lax.axis_size("ctx")
    return lax.ppermute(
        x, AXES, [(d * ctx + a, d * ctx + b) for d in range(lax.axis_size("dp")) for a, b in steps]
    )


def inner():
    z = lax.axis_index("ctx")
    return (z == 1) | (z == 2)


def gather_line(x):
    if lax.axis_size("ctx") != 4:
        return gather(x, [("ctx", b) for b in range(bits_of(lax.axis_size("ctx")))])
    pair = gather(x, [("ctx", 0)])
    middle = send_ctx(pair, ((1, 2), (2, 1)))
    outer = send_ctx(middle, ((1, 0), (2, 3)))
    return join(pair, jnp.where(inner(), middle, outer), my_bit(("ctx", 1)), 0)


def scatter_line(x):
    if lax.axis_size("ctx") != 4:
        return scatter(x, [("ctx", b) for b in range(bits_of(lax.axis_size("ctx")))][::-1])
    side = my_bit(("ctx", 1))
    far = lax.dynamic_index_in_dim(x, 1 - side, 0, keepdims=False)
    near = lax.dynamic_index_in_dim(x, side, 0, keepdims=False)
    passed = send_ctx(far, ((0, 1), (3, 2)))
    far = (far.astype(F32) + passed.astype(F32)).astype(BF16)
    crossed = send_ctx(far, ((1, 2), (2, 1)))
    near = (near.astype(F32) + crossed.astype(F32)).astype(BF16)
    return scatter(near, [("ctx", 0)])


def after(x, *others):
    return lax.optimization_barrier((x, *others))[0]


def normalize(values):
    center = jnp.mean(values, axis=-1, keepdims=True)
    offsets = values - center
    spread = jnp.mean(offsets * offsets, axis=-1, keepdims=True)
    scale = lax.rsqrt(spread + 1e-05)
    return offsets * scale, scale


def norm_back(grad, gain, hat, scale):
    e = grad * gain
    return scale * (
        e
        - jnp.mean(e, axis=-1, keepdims=True)
        - hat * jnp.mean(e * hat, axis=-1, keepdims=True)
    )


def gelu_tanh(values):
    return jax.nn.gelu(values, approximate=True)


def per_device(
    layer_input,
    prefix,
    ln1_gain,
    ln1_bias,
    w_qkv,
    b_qv,
    w_out,
    b_out,
    ln2_gain,
    ln2_bias,
    w_up,
    b_up,
    w_down,
    b_down,
    cotangent,
):
    dp, ctx = lax.axis_size("dp"), lax.axis_size("ctx")
    devices = dp * ctx
    planes = dp // 2
    tokens, d = layer_input.shape[1:]
    length = tokens * ctx
    width = HEADS * HD // ctx
    ff = b_up.shape[0] * devices
    units = ff // planes
    piece = b_up.shape[0]
    rows = d // devices
    core_bit = ("dp", 0)
    plane_bits = [("dp", b) for b in range(1, bits_of(dp))]
    ctx_bits = [("ctx", b) for b in range(bits_of(ctx))]
    twos = lambda bits: (2,) * len(bits)
    core = my_bit(core_bit)
    z = lax.axis_index("ctx")
    x_own = layer_input[0]
    cot_own = cotangent[0]

    small = [ln1_gain, ln1_bias, b_qv, b_out, ln2_gain, ln2_bias, b_up, b_down]
    sizes = [s.shape[0] for s in small]
    placed = [
        jnp.where(jnp.arange(size * ctx) // size == z, jnp.tile(v, ctx), 0)
        for v, size in zip(small, sizes)
    ]
    share = sum(sizes) * ctx
    extra = -(-share // (128 * rows)) * 128
    placed = jnp.concatenate(placed + [jnp.zeros((rows * extra - share,), BF16)]).reshape(rows, extra)
    by_head = w_qkv.reshape(rows, 3, ctx, width)
    take = lambda j: jnp.concatenate(
        [
            lax.dynamic_index_in_dim(by_head, j, 2, keepdims=False).reshape(rows, 3 * width),
            placed,
            w_out,
        ],
        1,
    )
    own_cols = jnp.stack(exchange_ctx(take), 0)
    wide = gather(own_cols, plane_bits + [core_bit])
    wide = wide.reshape(dp, ctx, rows, 3 * width + extra + d)
    proj_qkv = wide[..., : 3 * width].reshape(d, 3 * width)
    proj_out = wide[..., 3 * width + extra :].reshape(d, d)
    shares = wide[..., 3 * width : 3 * width + extra].astype(F32)
    shares = jnp.sum(shares, axis=1).reshape(dp, rows * extra)
    whole = []
    start = 0
    for size in sizes:
        whole.append(shares[:, start : start + size * ctx].reshape(devices * size))
        start += size * ctx
    gain_first, shift_first, bias_qv, bias_out, gain_second, shift_second, bias_up, bias_down = whole

    inputs_all = jnp.concatenate(gather_ctx(after(x_own, own_cols)), 0)

    orders = (plane_bits, plane_bits[::-1])
    up_rows = jnp.stack(
        exchange_planes(lambda p: lax.dynamic_slice_in_dim(w_up, p * units, units, 1)), 0
    )
    lines_up = gather_line(up_rows).reshape(ctx, planes, rows, units).transpose(1, 0, 2, 3)
    proj_up = join(lines_up, swap(lines_up, core_bit), core, 1).reshape(d, units)
    lines_down = gather_line(after(w_down, inputs_all))
    proj_down = join(lines_down, swap(lines_down, core_bit), core, 0).reshape(units, d)
    bias_up_own = lax.dynamic_slice_in_dim(bias_up, (lax.axis_index("dp") >> 1) * units, units, 0)
    cot_pool = pool_rows(after(cot_own, wide), orders)

    hat_all, scale_all = normalize(inputs_all.astype(F32))
    hidden_first = (hat_all * gain_first + shift_first).astype(BF16)
    mixed = jnp.dot(hidden_first, proj_qkv, preferred_element_type=F32)
    bias_heads = lax.dynamic_index_in_dim(bias_qv.reshape(2, ctx, width), z, 1, keepdims=False)
    bias_mixed = jnp.concatenate([bias_heads[0], jnp.zeros((width,), F32), bias_heads[1]])
    mixed = (mixed + bias_mixed).astype(BF16)
    attended_heads, log_total = attention(prefix, mixed)
    attended = jnp.concatenate(
        exchange_ctx(lambda j: lax.dynamic_slice_in_dim(attended_heads, j * tokens, tokens, 0)), 1
    )

    inputs = x_own.astype(F32)
    resid = inputs + jnp.dot(attended, proj_out, preferred_element_type=F32) + bias_out
    hat_second, scale_second = normalize(resid)
    hidden_second = (hat_second * gain_second + shift_second).astype(BF16)

    hidden_pool = pool_rows(hidden_second, orders)
    pre_act = jnp.dot(hidden_pool, proj_up, preferred_element_type=F32) + bias_up_own
    gelu_value, gelu_pull = jax.vjp(gelu_tanh, pre_act)
    activ = gelu_value.astype(BF16)
    grad_activ = dot_nt(cot_pool, proj_down)
    grad_pre = gelu_pull(grad_activ)[0].astype(BF16)
    grad_hidden_second = share_rows(dot_nt(grad_pre, proj_up), orders)
    out_part = dot_nn(after(activ, grad_hidden_second), proj_down)
    layer_out = (resid + share_rows(out_part, orders) + bias_down).astype(BF16)

    upstream = cot_own.astype(F32)
    grad_gain_second = jnp.sum(grad_hidden_second * hat_second, axis=0)
    grad_shift_second = jnp.sum(grad_hidden_second, axis=0)
    grad_resid = upstream + norm_back(grad_hidden_second, gain_second, hat_second, scale_second)
    grad_branch = grad_resid.astype(BF16)
    grad_bias_out = jnp.sum(grad_branch.astype(F32), axis=0)
    grad_attended = dot_nt(grad_branch, proj_out).astype(BF16)
    grad_heads = jnp.concatenate(
        exchange_ctx(lambda j: lax.dynamic_slice_in_dim(grad_attended, j * width, width, 1)), 0
    )

    grad = dot_tn(activ, cot_pool).astype(BF16)
    grad = grad.reshape((2,) + twos(ctx_bits) + (piece, d))
    sum_down = scatter_line(scatter(grad, [core_bit], ctx_bits, BF16))
    grad = dot_tn(hidden_pool, grad_pre).astype(BF16)
    grad = grad.reshape(planes, 2, ctx, rows, units).transpose(1, 2, 0, 3, 4)
    grad = grad.reshape((2,) + twos(ctx_bits) + (planes, rows, units))
    up_sum = scatter_line(scatter(grad, [core_bit], ctx_bits, BF16)).astype(BF16)
    columns = exchange_planes(lambda p: lax.dynamic_index_in_dim(up_sum, p, 0, keepdims=False))
    sum_up = jnp.concatenate(columns, 1).astype(F32)

    grad_out = dot_tn(attended, grad_branch).astype(BF16)
    grad_out = grad_out.reshape(twos(plane_bits) + (2,) + twos(ctx_bits) + (rows, d))
    grad_out = scatter(grad_out, [core_bit] + plane_bits, ctx_bits, BF16)
    sum_out = scatter_line(grad_out)

    grad_q, grad_k, grad_v = attention_grads(prefix, mixed, attended_heads, grad_heads, log_total)
    grad_mixed = jnp.concatenate([grad_q, grad_k, grad_v], 1)
    grad_hidden_all = dot_nt(grad_mixed, proj_qkv)
    grad_gain_first = jnp.sum(grad_hidden_all * hat_all, axis=0)
    grad_shift_first = jnp.sum(grad_hidden_all, axis=0)
    grad_hidden_low = grad_hidden_all.astype(BF16)
    grad_hidden_first = sum_ctx(
        lambda j: lax.dynamic_slice_in_dim(grad_hidden_low, j * tokens, tokens, 0)
    )
    hat_first, scale_first = normalize(inputs)
    input_grad = grad_resid + norm_back(grad_hidden_first, gain_first, hat_first, scale_first)

    grad_qkv = dot_tn(hidden_first, grad_mixed).astype(BF16)
    grad_qkv = grad_qkv.reshape((2,) * bits_of(dp) + (ctx * rows, 3 * width))
    own_rows = scatter(grad_qkv, [core_bit] + plane_bits, (), BF16).reshape(ctx, rows, 3 * width)
    columns = exchange_ctx(lambda j: lax.dynamic_index_in_dim(own_rows, j, 0, keepdims=False))
    sum_qkv = (
        jnp.stack([c.reshape(rows, 3, width) for c in columns], 2)
        .reshape(rows, 3 * d)
        .astype(F32)
    )

    sums_heads = jnp.sum(grad_mixed.astype(F32), axis=0).reshape(3, width)
    at_heads = lambda t: jnp.where(jnp.arange(d) // width == z, jnp.tile(t, ctx), 0)
    grad_bias_qv = jnp.concatenate([at_heads(sums_heads[0]), at_heads(sums_heads[2])])
    up_units = jnp.sum(grad_pre.astype(F32), axis=0)[None]
    here = jnp.arange(planes)[:, None] == lax.axis_index("dp") >> 1
    grad_bias_up = jnp.where(here, up_units, 0)
    grads = [
        grad_gain_first,
        grad_shift_first,
        grad_bias_qv,
        grad_bias_out,
        grad_gain_second,
        grad_shift_second,
        grad_bias_up,
        jnp.sum(upstream, axis=0),
    ]
    packed = jnp.concatenate([g.reshape(dp, size * ctx) for g, size in zip(grads, sizes)], 1)
    packed = packed.reshape((2,) * bits_of(dp) + (share,))
    packed = scatter(packed, plane_bits + [core_bit])
    packed = packed + sum(swap_by(packed, 0, s) for s in range(1, ctx))
    sums = []
    start = 0
    for size in sizes:
        sums.append(lax.dynamic_slice_in_dim(packed, start + z * size, size, 0))
        start += size * ctx
    (
        sum_gain_first,
        sum_shift_first,
        sum_bias_qv,
        sum_bias_out,
        sum_gain_second,
        sum_shift_second,
        sum_bias_up,
        sum_bias_down,
    ) = sums
    return (
        layer_out[None],
        input_grad[None],
        sum_gain_first,
        sum_shift_first,
        sum_qkv,
        sum_bias_qv,
        sum_out,
        sum_bias_out,
        sum_gain_second,
        sum_shift_second,
        sum_up,
        sum_bias_up,
        sum_down,
        sum_bias_down,
    )


def solution(mesh):
    vector = P(AXES)
    matrix = P(AXES, None)
    tokens = P("dp", "ctx", None)
    return jax.shard_map(
        per_device,
        mesh=mesh,
        in_specs=(
            tokens,
            P("dp"),
            vector,
            vector,
            matrix,
            vector,
            matrix,
            vector,
            vector,
            vector,
            matrix,
            vector,
            matrix,
            vector,
            tokens,
        ),
        out_specs=(
            tokens,
            tokens,
            vector,
            vector,
            matrix,
            vector,
            matrix,
            vector,
            vector,
            vector,
            matrix,
            vector,
            matrix,
            vector,
        ),
        check_vma=False,
    )
```

```python
import functools

import jax
import jax.numpy as jnp
from jax import lax
from jax.experimental import pallas as pl
from jax.experimental.pallas import tpu as pltpu
from jax.sharding import PartitionSpec as P

HEADS = 16
HD = 64
SCALE = 0.125
NEGATIVE = -1e30
AXES = ("dp", "ctx")
F32 = jnp.float32
BF16 = jnp.bfloat16


def dot_nt(a, b):
    return lax.dot_general(a, b, (((1,), (1,)), ((), ())), preferred_element_type=F32)


def dot_tn(a, b):
    return lax.dot_general(a, b, (((0,), (0,)), ((), ())), preferred_element_type=F32)


def dot_nn(a, b):
    return lax.dot_general(a, b, (((1,), (0,)), ((), ())), preferred_element_type=F32)


def allowed_keys(limit, rows, first_query, prefix_len):
    key_pos = lax.broadcasted_iota(jnp.int32, (limit, rows), 0)
    query_pos = lax.broadcasted_iota(jnp.int32, (limit, rows), 1) + first_query
    return (key_pos <= query_pos) | (key_pos < prefix_len)


def over_blocks(length, rows, step):
    if length <= 1024:
        for first in range(0, length, rows):
            step(first, max(length // 2, first + rows))
    else:

        def body(i, carry):
            step(pl.multiple_of(i * rows, rows), length)
            return carry

        lax.fori_loop(0, length // rows, body, 0)


def attend_forward(prefix_ref, q_ref, k_ref, v_ref, o_ref, lse_ref, *, rows):
    length, width = q_ref.shape
    group = width // HD
    prefix_len = prefix_ref[0]
    lane_head = lax.broadcasted_iota(jnp.int32, (1, width), 1) // HD

    def step(first, limit):
        block = pl.ds(first, rows)
        queries = q_ref[block, :] * SCALE
        keys = k_ref[:limit, :]
        values = v_ref[:limit, :]
        allowed = allowed_keys(limit, rows, first, prefix_len)
        attended = jnp.zeros((rows, width), F32)
        for h in range(group):
            mine = lane_head == h
            scores = dot_nt(keys, jnp.where(mine, queries, 0).astype(BF16))
            scores = jnp.where(allowed, scores, NEGATIVE)
            top = jnp.max(scores, axis=0, keepdims=True)
            terms = jnp.exp(scores - top)
            total = jnp.sum(terms, axis=0, keepdims=True)
            lse_ref[h, :, block] = top + jnp.log(total)
            weights = (terms * (1.0 / total)).astype(BF16)
            attended = jnp.where(mine, dot_tn(weights, values), attended)
        o_ref[block, :] = attended.astype(BF16)

    over_blocks(length, rows, step)


def attend_backward(
    prefix_ref, q_ref, k_ref, v_ref, o_ref, do_ref, lse_ref, dq_ref, dk_ref, dv_ref, dk_sum, dv_sum, *, rows
):
    length, width = q_ref.shape
    group = width // HD
    prefix_len = prefix_ref[0]
    lane_head = lax.broadcasted_iota(jnp.int32, (1, width), 1) // HD
    dk_sum[...] = jnp.zeros_like(dk_sum)
    dv_sum[...] = jnp.zeros_like(dv_sum)

    def step(first, limit):
        block = pl.ds(first, rows)
        queries = q_ref[block, :] * SCALE
        grads = do_ref[block, :]
        keys = k_ref[:limit, :]
        values = v_ref[:limit, :]
        allowed = allowed_keys(limit, rows, first, prefix_len)
        products = (grads.astype(F32) * o_ref[block, :].astype(F32)).T
        query_grad = jnp.zeros((rows, width), F32)
        for h in range(group):
            mine = lane_head == h
            queries_h = jnp.where(mine, queries, 0).astype(BF16)
            grads_h = jnp.where(mine, grads, 0).astype(BF16)
            delta = jnp.sum(products[h * HD : (h + 1) * HD, :], axis=0, keepdims=True)
            scores = jnp.where(allowed, dot_nt(keys, queries_h), NEGATIVE)
            probs = jnp.exp(scores - lse_ref[h, :, block])
            weight_grad = dot_nt(values, grads_h)
            score_grad = (probs * (weight_grad - delta)).astype(BF16)
            dv_sum[:limit, :] += dot_nn(probs.astype(BF16), grads_h)
            dk_sum[:limit, :] += dot_nn(score_grad, queries_h)
            query_grad = jnp.where(mine, dot_tn(score_grad, keys), query_grad)
        dq_ref[block, :] = (query_grad * SCALE).astype(BF16)

    over_blocks(length, rows, step)
    dk_ref[...] = dk_sum[...].astype(BF16)
    dv_ref[...] = dv_sum[...].astype(BF16)


def attention_shapes(mixed):
    length, width = mixed.shape
    heads = width // (3 * HD)
    group = 2 if heads % 2 == 0 else 1
    return length, heads, group, heads // group, group * HD


def thirds(mixed, count, lanes):
    length, width = mixed.shape
    part = lambda n: pl.BlockSpec((length, lanes), lambda g: (0, n * count + g))
    if lanes % 128 == 0:
        return [mixed] * 3, [part(0), part(1), part(2)]
    return [mixed[:, n * width // 3 : (n + 1) * width // 3] for n in range(3)], [part(0)] * 3


def attention(prefix, mixed):
    length, heads, group, count, lanes = attention_shapes(mixed)
    operands, columns = thirds(mixed, count, lanes)
    return pl.pallas_call(
        functools.partial(attend_forward, rows=min(256, length)),
        grid=(count,),
        in_specs=[pl.BlockSpec(memory_space=pltpu.SMEM)] + columns,
        out_specs=[
            pl.BlockSpec((length, lanes), lambda g: (0, g)),
            pl.BlockSpec((group, 1, length), lambda g: (g, 0, 0)),
        ],
        out_shape=[
            jax.ShapeDtypeStruct((length, heads * HD), BF16),
            jax.ShapeDtypeStruct((heads, 1, length), F32),
        ],
        compiler_params=pltpu.CompilerParams(vmem_limit_bytes=48 * 2**20),
        name="attend_forward",
    )(prefix, *operands)


def attention_grads(prefix, mixed, attended, grad_attended, log_total):
    length, heads, group, count, lanes = attention_shapes(mixed)
    operands, columns = thirds(mixed, count, lanes)
    own = pl.BlockSpec((length, lanes), lambda g: (0, g))
    wide = jax.ShapeDtypeStruct((length, heads * HD), BF16)
    return pl.pallas_call(
        functools.partial(attend_backward, rows=min(256, length)),
        grid=(count,),
        in_specs=[
            pl.BlockSpec(memory_space=pltpu.SMEM),
            *columns,
            own,
            own,
            pl.BlockSpec((group, 1, length), lambda g: (g, 0, 0)),
        ],
        out_specs=[own] * 3,
        out_shape=[wide] * 3,
        scratch_shapes=[pltpu.VMEM((length, lanes), F32)] * 2,
        compiler_params=pltpu.CompilerParams(vmem_limit_bytes=48 * 2**20),
        name="attend_backward",
    )(prefix, *operands, attended, grad_attended, log_total)


def norm_project(place_ref, *refs, count):
    x_refs, refs = refs[:count], refs[count:]
    own_ref, other_ref, gain_ref, shift_ref, bias_ref, hidden_ref, mixed_ref, w_buf = refs
    tokens = x_refs[0].shape[0]
    columns = bias_ref.shape[1]
    core = place_ref[1]
    planes, rows = own_ref.shape[:2]
    for p in range(planes):
        for c, source in ((core, own_ref), (1 - core, other_ref)):
            into = pl.ds(pl.multiple_of((2 * p + c) * rows, rows), rows)
            w_buf[into, :] = source[p, :, :columns]
    for s, x_ref in enumerate(x_refs):
        values = x_ref[...].astype(F32)
        offsets = values - jnp.mean(values, axis=-1, keepdims=True)
        spread = jnp.mean(offsets * offsets, axis=-1, keepdims=True)
        hidden = offsets * lax.rsqrt(spread + 1e-05) * gain_ref[...] + shift_ref[...]
        hidden = hidden.astype(BF16)
        block = pl.ds(pl.multiple_of((place_ref[0] ^ s) * tokens, tokens), tokens)
        hidden_ref[block, :] = hidden
        mixed_ref[block, :] = (dot_nn(hidden, w_buf[...]) + bias_ref[...]).astype(BF16)


def norm_and_project(place, pieces, own, other, gain, shift, bias):
    tokens, d = pieces[0].shape
    count = len(pieces)
    vmem = pl.BlockSpec(memory_space=pltpu.VMEM)
    return pl.pallas_call(
        functools.partial(norm_project, count=count),
        in_specs=[pl.BlockSpec(memory_space=pltpu.SMEM)] + [vmem] * (count + 5),
        out_specs=[vmem, vmem],
        out_shape=[
            jax.ShapeDtypeStruct((tokens * count, d), BF16),
            jax.ShapeDtypeStruct((tokens * count, bias.shape[0]), BF16),
        ],
        scratch_shapes=[pltpu.VMEM((d, bias.shape[0]), BF16)],
        compiler_params=pltpu.CompilerParams(vmem_limit_bytes=48 * 2**20),
        name="norm_project",
    )(place, *pieces, own, other, gain[None], shift[None], bias[None])


def pack_messages(here_ref, w_ref, out_ref, *refs, sizes, width, extra):
    small, sends = refs[: len(sizes)], refs[len(sizes) :]
    count = len(sends)
    rows, d = out_ref.shape
    here = here_ref[0]
    row = lax.broadcasted_iota(jnp.int32, (rows, extra), 0)
    lane = lax.broadcasted_iota(jnp.int32, (rows, extra), 1)
    flat = row * extra + lane
    placed = jnp.zeros((rows, extra), F32)
    start = 0
    for v_ref, size in zip(small, sizes):
        spread = lax.broadcasted_iota(jnp.int32, (size, extra), 1) % size
        spread = spread == lax.broadcasted_iota(jnp.int32, (size, extra), 0)
        repeated = dot_nn(v_ref[...], jnp.where(spread, 1.0, 0.0).astype(BF16))
        first = start + here * size
        placed = jnp.where((flat >= first) & (flat < first + size), repeated, placed)
        start += size * count
    placed = placed.astype(BF16)
    for s, send_ref in enumerate(sends):
        to = here ^ s
        for part in range(3):
            columns = pl.ds(pl.multiple_of(part * d + to * width, 128), width)
            send_ref[:, part * width : (part + 1) * width] = w_ref[:, columns]
        send_ref[:, 3 * width : 3 * width + extra] = placed
        send_ref[:, 3 * width + extra :] = out_ref[...]


def first_messages(here, w_qkv, w_out, small, sizes, width, extra, count):
    rows, d = w_out.shape
    vmem = pl.BlockSpec(memory_space=pltpu.VMEM)
    return pl.pallas_call(
        functools.partial(pack_messages, sizes=sizes, width=width, extra=extra),
        in_specs=[pl.BlockSpec(memory_space=pltpu.SMEM)] + [vmem] * (2 + len(small)),
        out_specs=[vmem] * count,
        out_shape=[jax.ShapeDtypeStruct((rows, 3 * width + extra + d), BF16)] * count,
        compiler_params=pltpu.CompilerParams(vmem_limit_bytes=48 * 2**20),
        name="first_messages",
    )(here[None], w_qkv, w_out, *[v[None] for v in small])


def feed_up(x_ref, w_ref, b_ref, activ_ref, slope_ref):
    u = dot_nn(x_ref[...], w_ref[...]) + b_ref[...]
    root = 0.7978845608028654
    cube = 0.044715 * root
    square = u * u
    t = jnp.tanh(u * (root + cube * square))
    half = 0.5 + 0.5 * t
    activ = u * half
    activ_ref[...] = activ.astype(BF16)
    slope_ref[...] = half + activ * (1.0 - t) * (root + (3.0 * cube) * square)


def feed_back(cot_ref, slope_ref, down_ref, up_ref, grad_ref, sums_ref, hidden_ref):
    grad = (dot_nt(cot_ref[...], down_ref[...]) * slope_ref[...]).astype(BF16)
    grad_ref[...] = grad

    @pl.when(pl.program_id(0) == 0)
    def _():
        sums_ref[...] = jnp.zeros_like(sums_ref)

    sums_ref[...] += jnp.sum(grad.astype(F32), axis=0, keepdims=True)
    hidden_ref[...] = dot_nt(grad, up_ref[...]).astype(BF16)


def up_and_gelu(hidden, proj_up, bias):
    rows, d = hidden.shape
    units = proj_up.shape[1]
    block = min(256, rows)
    by_rows = lambda n: pl.BlockSpec((block, n), lambda i: (i, 0))
    whole = lambda m, n: pl.BlockSpec((m, n), lambda i: (0, 0))
    return pl.pallas_call(
        feed_up,
        grid=(rows // block,),
        in_specs=[by_rows(d), whole(d, units), whole(1, units)],
        out_specs=[by_rows(units), by_rows(units)],
        out_shape=[
            jax.ShapeDtypeStruct((rows, units), BF16),
            jax.ShapeDtypeStruct((rows, units), F32),
        ],
        compiler_params=pltpu.CompilerParams(vmem_limit_bytes=48 * 2**20),
        name="feed_up",
    )(hidden, proj_up, bias[None])


def hidden_grads(cot, slope, proj_down, proj_up):
    rows, units = slope.shape
    d = cot.shape[1]
    block = min(256, rows)
    by_rows = lambda n: pl.BlockSpec((block, n), lambda i: (i, 0))
    whole = lambda m, n: pl.BlockSpec((m, n), lambda i: (0, 0))
    return pl.pallas_call(
        feed_back,
        grid=(rows // block,),
        in_specs=[by_rows(d), by_rows(units), whole(units, d), whole(d, units)],
        out_specs=[by_rows(units), whole(1, units), by_rows(d)],
        out_shape=[
            jax.ShapeDtypeStruct((rows, units), BF16),
            jax.ShapeDtypeStruct((1, units), F32),
            jax.ShapeDtypeStruct((rows, d), BF16),
        ],
        compiler_params=pltpu.CompilerParams(vmem_limit_bytes=48 * 2**20),
        name="feed_back",
    )(cot, slope, proj_down, proj_up)


def bits_of(size):
    return size.bit_length() - 1


def rank(bit):
    return (0 if bit[0] == "ctx" else 1, bit[1])


def my_bit(bit):
    return (lax.axis_index(bit[0]) >> bit[1]) & 1


def swap_by(x, dp_mask, ctx_mask):
    dp, ctx = lax.axis_size("dp"), lax.axis_size("ctx")
    pairs = [
        (d * ctx + c, (d ^ dp_mask) * ctx + (c ^ ctx_mask)) for d in range(dp) for c in range(ctx)
    ]
    return lax.ppermute(x, AXES, pairs)


def swap(x, bit):
    return swap_by(x, 1 << bit[1], 0) if bit[0] == "dp" else swap_by(x, 0, 1 << bit[1])


def join(own, other, here, axis):
    first = here == 0
    return jnp.stack([jnp.where(first, own, other), jnp.where(first, other, own)], axis)


class Steps:
    def __init__(self, generator):
        self.generator = generator
        self.pending = None
        self.result = None
        self.move(None)

    def move(self, arrived):
        try:
            self.pending = self.generator.send(arrived)
        except StopIteration as stop:
            self.pending = None
            self.result = stop.value

    def finish(self):
        while self.pending is not None:
            self.move(self.pending)
        return self.result


def meet(steps, *values, held=()):
    both = [(s, True) for s in steps if s.pending is not None]
    both += [(s, False) for s in held if s.pending is not None]
    flat = [p for s, _ in both for p in s.pending]
    flat = lax.optimization_barrier((*flat, *values))
    start = 0
    for s, moves in both:
        count = len(s.pending)
        s.pending = list(flat[start : start + count])
        if moves:
            s.move(s.pending)
        start += count
    values = flat[start:]
    return values[0] if len(values) == 1 else values


def gather(x, bits, done=()):
    done = list(done)
    for bit in bits:
        place = sum(rank(d) > rank(bit) for d in done)
        (other,) = yield [swap(x, bit)]
        x = join(x, other, my_bit(bit), place)
        done.append(bit)
    return x


def scatter(x, bits, left=(), last=F32):
    remaining = sorted(list(bits) + list(left), key=rank, reverse=True)
    for n, bit in enumerate(bits):
        place = remaining.index(bit)
        here = my_bit(bit)
        sent = lax.dynamic_index_in_dim(x, 1 - here, place, keepdims=False)
        kept = lax.dynamic_index_in_dim(x, here, place, keepdims=False)
        (other,) = yield [swap(sent, bit)]
        x = kept.astype(F32) + other.astype(F32)
        remaining.pop(place)
        x = x.astype(sent.dtype if n + 1 < len(bits) else last)
    return x


def exchange(x, bits):
    remaining = sorted(bits, key=rank, reverse=True)
    done = []
    for bit in bits:
        place = remaining.index(bit)
        here = my_bit(bit)
        sent = lax.dynamic_index_in_dim(x, 1 - here, place, keepdims=False)
        kept = lax.dynamic_index_in_dim(x, here, place, keepdims=False)
        (other,) = yield [swap(sent, bit)]
        remaining.pop(place)
        place = len(remaining) + sum(rank(d) > rank(bit) for d in done)
        x = join(kept, other, here, place)
        done.append(bit)
    return x


def pool_rows(x, orders):
    count = x.shape[0] // 2
    parts = [x[:count][None], x[count:][None]]
    for bits in zip(*orders):
        others = yield [swap(part, bit) for part, bit in zip(parts, bits)]
        parts = [jnp.concatenate(both, 0) for both in zip(parts, others)]
    return jnp.concatenate(parts, 0).reshape(-1, x.shape[1])


def share_rows(x, orders):
    planes = 2 ** len(orders[0])
    x = x.reshape(2, planes, x.shape[0] // (2 * planes), x.shape[1])
    parts = [x[0], x[1]]
    for bits in zip(*(order[::-1] for order in orders)):
        count = parts[0].shape[0] // 2
        others = yield [swap(part[count:].astype(BF16), bit) for part, bit in zip(parts, bits)]
        parts = [p[:count].astype(F32) + o.astype(F32) for p, o in zip(parts, others)]
    return jnp.concatenate([p[0] for p in parts], 0)


def unrelate(pieces, me):
    for b in range(bits_of(len(pieces))):
        flip = ((me >> b) & 1) == 1
        pieces = [jnp.where(flip, pieces[j ^ (1 << b)], pieces[j]) for j in range(len(pieces))]
    return pieces


def send_others(pick):
    me = lax.axis_index("ctx")
    return [swap_by(pick(me ^ s), 0, s) for s in range(1, lax.axis_size("ctx"))]


def send_ctx(x, steps):
    ctx = lax.axis_size("ctx")
    return lax.ppermute(
        x, AXES, [(d * ctx + a, d * ctx + b) for d in range(lax.axis_size("dp")) for a, b in steps]
    )


def inner():
    z = lax.axis_index("ctx")
    return (z == 1) | (z == 2)


def ctx_bits_of():
    return [("ctx", b) for b in range(bits_of(lax.axis_size("ctx")))]


def gather_line(x):
    if lax.axis_size("ctx") != 4:
        return (yield from gather(x, ctx_bits_of()))
    pair = yield from gather(x, [("ctx", 0)])
    (middle,) = yield [send_ctx(pair, ((1, 2), (2, 1)))]
    (outer,) = yield [send_ctx(middle, ((1, 0), (2, 3)))]
    return join(pair, jnp.where(inner(), middle, outer), my_bit(("ctx", 1)), 0)


def scatter_line(x):
    if lax.axis_size("ctx") != 4:
        return (yield from scatter(x, ctx_bits_of()[::-1]))
    side = my_bit(("ctx", 1))
    far = lax.dynamic_index_in_dim(x, 1 - side, 0, keepdims=False)
    near = lax.dynamic_index_in_dim(x, side, 0, keepdims=False)
    (passed,) = yield [send_ctx(far, ((0, 1), (3, 2)))]
    far = (far.astype(F32) + passed.astype(F32)).astype(BF16)
    (crossed,) = yield [send_ctx(far, ((1, 2), (2, 1)))]
    near = (near.astype(F32) + crossed.astype(F32)).astype(BF16)
    return (yield from scatter(near, [("ctx", 0)]))


def slot_masks(bits):
    masks = [0]
    for bit in bits:
        masks += [m | 1 << bit[1] for m in masks]
    return masks


def in_pool_order(x, orders):
    planes, count, columns = x.shape
    first = slot_masks(orders[0])
    blocks = []
    for h, bits in enumerate(orders):
        for mask in slot_masks(bits):
            part = x[first.index(mask)]
            blocks.append(part[h * count // 2 : (h + 1) * count // 2])
    return jnp.concatenate(blocks, 0)


def in_chain_order(x, orders):
    planes = 2 ** len(orders[0])
    x = x.reshape(2, planes, -1, x.shape[1])
    places = [slot_masks(bits) for bits in orders]
    return jnp.stack(
        [jnp.concatenate([x[h, places[h].index(m)] for h in range(2)], 0) for m in places[0]], 0
    )


def share_chain(x, bits):
    for bit in bits[::-1]:
        count = x.shape[0] // 2
        (other,) = yield [swap(x[count:].astype(BF16), bit)]
        x = x[:count].astype(F32) + other.astype(F32)
    return x[0]


def pool_chain(x, bits):
    x = x[None]
    for bit in bits:
        (other,) = yield [swap(x, bit)]
        x = jnp.concatenate([x, other], 0)
    return x


def plane_exchange(x):
    bits = [("dp", b) for b in range(1, bits_of(lax.axis_size("dp")))]
    y = yield from exchange(x.reshape((2,) * len(bits) + x.shape[1:]), bits)
    return y.reshape(x.shape)


def core_then_line(x):
    x = yield from scatter(x, [("dp", 0)], ctx_bits_of(), BF16)
    return (yield from scatter_line(x))


def sum_planes(x):
    me = lax.axis_index("dp") >> 1
    pick = lambda p: lax.dynamic_index_in_dim(x, p, 0, keepdims=False)
    others = yield [swap_by(pick(me ^ s), s << 1, 0) for s in range(1, x.shape[0])]
    return pick(me).astype(F32) + sum(o.astype(F32) for o in others)


def other_core(x):
    (other,) = yield [swap(x, ("dp", 0))]
    return other


def pair_step(x):
    if lax.axis_size("ctx") != 4:
        return x
    return (yield from gather(x, [("ctx", 0)]))


def rest_then_core(x):
    if lax.axis_size("ctx") != 4:
        x = yield from gather(x, ctx_bits_of())
    else:
        (middle,) = yield [send_ctx(x, ((1, 2), (2, 1)))]
        (outer,) = yield [send_ctx(middle, ((1, 0), (2, 3)))]
        x = join(x, jnp.where(inner(), middle, outer), my_bit(("ctx", 1)), 0)
    (other,) = yield [swap(x, ("dp", 0))]
    return x, other


def core_line_planes(x):
    x = yield from core_then_line(x)
    return (yield from plane_exchange(x.astype(BF16)))


def normalize(values):
    center = jnp.mean(values, axis=-1, keepdims=True)
    offsets = values - center
    spread = jnp.mean(offsets * offsets, axis=-1, keepdims=True)
    scale = lax.rsqrt(spread + 1e-05)
    return offsets * scale, scale


def norm_back(grad, gain, hat, scale):
    e = grad * gain
    return scale * (
        e
        - jnp.mean(e, axis=-1, keepdims=True)
        - hat * jnp.mean(e * hat, axis=-1, keepdims=True)
    )


def gelu_tanh(values):
    return jax.nn.gelu(values, approximate=True)


def per_device(
    layer_input,
    prefix,
    ln1_gain,
    ln1_bias,
    w_qkv,
    b_qv,
    w_out,
    b_out,
    ln2_gain,
    ln2_bias,
    w_up,
    b_up,
    w_down,
    b_down,
    cotangent,
):
    dp, ctx = lax.axis_size("dp"), lax.axis_size("ctx")
    devices = dp * ctx
    planes = dp // 2
    tokens, d = layer_input.shape[1:]
    length = tokens * ctx
    width = HEADS * HD // ctx
    ff = b_up.shape[0] * devices
    units = ff // planes
    piece = b_up.shape[0]
    rows = d // devices
    core_bit = ("dp", 0)
    plane_bits = [("dp", b) for b in range(1, bits_of(dp))]
    ctx_bits = [("ctx", b) for b in range(bits_of(ctx))]
    twos = lambda bits: (2,) * len(bits)
    core = my_bit(core_bit)
    z = lax.axis_index("ctx")
    x_own = layer_input[0]
    cot_own = cotangent[0]
    orders = (plane_bits, plane_bits[::-1])
    plane = lax.axis_index("dp") >> 1

    small = [ln1_gain, ln1_bias, b_qv, b_out, ln2_gain, ln2_bias, b_up, b_down]
    sizes = [s.shape[0] for s in small]
    share = sum(sizes) * ctx
    extra = -(-share // (128 * rows)) * 128
    early = 3 * width + extra
    if all(size * ctx % extra == 0 for size in sizes) and width % 128 == 0:
        sends = first_messages(z, w_qkv, w_out, small, sizes, width, extra, ctx)
    else:
        placed = [
            jnp.where(jnp.arange(size * ctx) // size == z, jnp.tile(v, ctx), 0)
            for v, size in zip(small, sizes)
        ]
        placed = jnp.concatenate(placed + [jnp.zeros((rows * extra - share,), BF16)])
        placed = placed.reshape(rows, extra)
        by_head = w_qkv.reshape(rows, 3, ctx, width)
        sends = []
        for s in range(ctx):
            own = lax.dynamic_index_in_dim(by_head, z ^ s, 2, keepdims=False)
            sends.append(jnp.concatenate([own.reshape(rows, 3 * width), placed, w_out], 1))
    columns = [sends[0]] + [swap_by(sends[s], 0, s) for s in range(1, ctx)]
    up_rows = Steps(plane_exchange(w_up.reshape(rows, planes, units).transpose(1, 0, 2)))
    cot = Steps(pool_chain(cot_own, plane_bits))
    *columns, x_now = meet([up_rows], *columns, x_own, held=[cot])
    columns = jnp.stack(unrelate(columns, z), 0)

    pieces = send_others(lambda j: x_now)
    qkv = Steps(gather(columns[..., :early], plane_bits))
    pieces[0], columns = meet([qkv, up_rows], pieces[0], columns)
    out = Steps(gather(columns[..., early:], plane_bits + [core_bit]))
    feed = jnp.stack([up_rows.finish().reshape(piece, d), w_down], 0)
    feed = Steps(pair_step(feed))
    pieces[1] = meet([qkv, out, feed, cot], pieces[1])
    own = qkv.finish().reshape(planes, ctx * rows, early)
    qkv = Steps(other_core(own))
    feed = feed.finish()
    feed = feed if ctx == 4 else feed[None]
    up = Steps(rest_then_core(feed[:, 0] if ctx == 4 else feed[0, 0]))
    pieces = meet([qkv], *pieces)
    other = qkv.finish()
    lane_part = lambda t: t[..., 3 * width :].reshape(planes, ctx, rows, extra).astype(F32)
    shares = join(jnp.sum(lane_part(own), 1), jnp.sum(lane_part(other), 1), core, 1)
    shares = shares.reshape(dp, rows * extra)
    whole = []
    start = 0
    for size in sizes:
        whole.append(shares[:, start : start + size * ctx].reshape(devices * size))
        start += size * ctx
    gain_first, shift_first, bias_qv, bias_out, gain_second, shift_second, bias_up, bias_down = whole

    bias_heads = lax.dynamic_index_in_dim(bias_qv.reshape(2, ctx, width), z, 1, keepdims=False)
    bias_mixed = jnp.concatenate([bias_heads[0], jnp.zeros((width,), F32), bias_heads[1]])
    inputs_all = [x_own, *pieces]
    place = jnp.stack([z, core]).astype(jnp.int32)
    hidden_first, mixed = norm_and_project(
        place, inputs_all, own, other, gain_first, shift_first, bias_mixed
    )
    attended_heads, log_total = attention(prefix, mixed)
    take = lambda j: lax.dynamic_slice_in_dim(attended_heads, j * tokens, tokens, 0)
    pieces = send_others(take)
    pieces[0], feed = meet([up, out], pieces[0], feed, held=[cot])
    down = Steps(rest_then_core(feed[:, 1] if ctx == 4 else feed[0, 1]))
    pieces[1] = meet([out], pieces[1])
    pieces = meet([], *pieces)
    attended = jnp.concatenate(unrelate([take(z), *pieces], z), 1)
    proj_out = out.finish().reshape(d, d)

    inputs = x_own.astype(F32)
    resid = inputs + jnp.dot(attended, proj_out, preferred_element_type=F32) + bias_out
    hat_second, scale_second = normalize(resid)
    hidden_second = (hat_second * gain_second + shift_second).astype(BF16)

    hidden = Steps(pool_rows(hidden_second, orders))
    meet([hidden, up, down])
    meet([hidden, up, down])
    across = lambda t: t.reshape(ctx, planes, rows, units).transpose(1, 0, 2, 3)
    lines, others = up.finish()
    proj_up = join(across(lines), across(others), core, 1).reshape(d, units)
    lines, others = down.finish()
    flat = lambda t: t.reshape(ctx, piece, d)
    proj_down = join(flat(lines), flat(others), core, 0).reshape(units, d)
    hidden_pool = hidden.finish()
    cot_pool = in_pool_order(cot.finish(), orders)
    bias_up_own = lax.dynamic_slice_in_dim(bias_up, plane * units, units, 0)
    activ, slope = up_and_gelu(hidden_pool, proj_up, bias_up_own)
    grad = dot_tn(activ, cot_pool).astype(BF16)
    grad, slope = meet([], grad, slope)
    down = Steps(core_then_line(grad.reshape((2,) + twos(ctx_bits) + (piece, d))))
    grad_pre, sums_pre, hidden_part = hidden_grads(cot_pool, slope, proj_down, proj_up)
    hidden_part, grad_pre = meet([], hidden_part, grad_pre)
    hidden = Steps(share_rows(hidden_part, orders))
    grad = dot_tn(hidden_pool, grad_pre).astype(BF16)
    grad = grad.reshape(planes, 2, ctx, rows, units).transpose(1, 2, 0, 3, 4)
    up = Steps(core_line_planes(grad.reshape((2,) + twos(ctx_bits) + (planes, rows, units))))
    meet([down])
    activ = meet([hidden, down], activ)
    out_part = dot_nn(activ, proj_down)
    out_part = meet([hidden, up], out_part)
    grad_hidden_second = hidden.finish()

    upstream = cot_own.astype(F32)
    grad_gain_second = jnp.sum(grad_hidden_second * hat_second, axis=0)
    grad_shift_second = jnp.sum(grad_hidden_second, axis=0)
    grad_resid = upstream + norm_back(grad_hidden_second, gain_second, hat_second, scale_second)
    grad_branch = grad_resid.astype(BF16)
    grad_bias_out = jnp.sum(grad_branch.astype(F32), axis=0)
    grad_attended = dot_nt(grad_branch, proj_out).astype(BF16)
    take = lambda j: lax.dynamic_slice_in_dim(grad_attended, j * width, width, 1)
    pieces = send_others(take)
    pieces[0] = meet([down, up], pieces[0])
    *pieces, grad_branch = meet([], *pieces, grad_branch)
    grad_heads = jnp.concatenate(unrelate([take(z), *pieces], z), 0)
    grad_q, grad_k, grad_v = attention_grads(prefix, mixed, attended_heads, grad_heads, log_total)
    grad_mixed = jnp.concatenate([grad_q, grad_k, grad_v], 1)
    wide_rows = join(own, other, core, 1)[..., : 3 * width].reshape(d, 3 * width)
    grad_hidden_all = dot_nt(grad_mixed, wide_rows)
    grad_hidden_low, grad_hidden_all, grad_mixed = meet(
        [], grad_hidden_all.astype(BF16), grad_hidden_all, grad_mixed, held=[down, up]
    )
    take = lambda j: lax.dynamic_slice_in_dim(grad_hidden_low, j * tokens, tokens, 0)
    pieces = send_others(take)
    rest = (grad_hidden_all, grad_mixed, hidden_first, attended, grad_branch, out_part)
    pieces[0], *rest, inputs_all[0] = meet([up], pieces[0], *rest, inputs_all[0], held=[down])
    grad_hidden_all, grad_mixed, hidden_first, attended, grad_branch, out_part = rest

    hat_all, _ = normalize(jnp.concatenate(unrelate(inputs_all, z), 0).astype(F32))
    sums_heads = jnp.sum(grad_mixed.astype(F32), axis=0).reshape(3, width)
    at_heads = lambda t: jnp.where(jnp.arange(d) // width == z, jnp.tile(t, ctx), 0)
    grads = [
        jnp.sum(grad_hidden_all * hat_all, axis=0),
        jnp.sum(grad_hidden_all, axis=0),
        jnp.concatenate([at_heads(sums_heads[0]), at_heads(sums_heads[2])]),
        grad_bias_out,
        grad_gain_second,
        grad_shift_second,
        jnp.where(jnp.arange(planes)[:, None] == plane, sums_pre, 0),
        jnp.sum(upstream, axis=0),
    ]
    packed = jnp.concatenate([g.reshape(dp, size * ctx) for g, size in zip(grads, sizes)], 1)
    packed = jnp.pad(packed.astype(BF16), ((0, 0), (0, rows * extra - share)))
    packed = jnp.pad(packed.reshape(dp, rows, extra), ((0, 0), (0, (ctx - 1) * rows), (0, 0)))
    grad_qkv = dot_tn(hidden_first, grad_mixed).astype(BF16).reshape(dp, ctx * rows, 3 * width)
    grad_qkv = jnp.concatenate([grad_qkv, packed], 2)
    grad_qkv = grad_qkv.reshape(twos(plane_bits) + (2, ctx * rows, early))
    qkv = Steps(scatter(grad_qkv, [core_bit] + plane_bits, (), BF16))
    grad_out = dot_tn(attended, grad_branch).astype(BF16)
    grad_out = grad_out.reshape(twos(plane_bits) + (2, ctx * rows, d))
    out = Steps(scatter(grad_out, [core_bit] + plane_bits[::-1], (), BF16))
    output = Steps(share_chain(in_chain_order(out_part, orders), plane_bits))
    meet([qkv])
    meet([out, up])
    pieces[1] = meet([qkv, out, up, output], pieces[1])
    sum_down = down.finish().reshape(piece, d)
    mine = qkv.finish()
    own_small = mine[:rows, 3 * width :]
    mine = mine[:, : 3 * width].reshape(ctx, rows, 3 * width)
    mine_out = out.finish().reshape(ctx, rows, d)

    take_last = lambda j: jnp.concatenate(
        [
            lax.dynamic_index_in_dim(mine, j, 0, keepdims=False),
            own_small,
            lax.dynamic_index_in_dim(mine_out, j, 0, keepdims=False),
        ],
        1,
    )
    layer_out = (resid + output.finish() + bias_down).astype(BF16)
    terms = [take_last(z)] + send_others(take_last)
    grad_hidden_first = take(z).astype(F32) + sum(p.astype(F32) for p in pieces)
    hat_first, scale_first = normalize(inputs)
    input_grad = grad_resid + norm_back(grad_hidden_first, gain_first, hat_first, scale_first)
    columns = unrelate([t[:, : 3 * width] for t in terms], z)
    sum_qkv = jnp.stack([c.reshape(rows, 3, width) for c in columns], 2)
    sum_qkv = sum_qkv.reshape(rows, 3 * d).astype(F32)
    sum_out = sum(t[:, early:].astype(F32) for t in terms)
    packed = sum(t[:, 3 * width : early].astype(F32) for t in terms).reshape(rows * extra)
    sum_up = up.finish().astype(F32).transpose(1, 0, 2).reshape(rows, ff)
    sums = []
    start = 0
    for size in sizes:
        sums.append(lax.dynamic_slice_in_dim(packed, start + z * size, size, 0))
        start += size * ctx
    (
        sum_gain_first,
        sum_shift_first,
        sum_bias_qv,
        sum_bias_out,
        sum_gain_second,
        sum_shift_second,
        sum_bias_up,
        sum_bias_down,
    ) = sums
    return (
        layer_out[None],
        input_grad[None],
        sum_gain_first,
        sum_shift_first,
        sum_qkv,
        sum_bias_qv,
        sum_out,
        sum_bias_out,
        sum_gain_second,
        sum_shift_second,
        sum_up,
        sum_bias_up,
        sum_down,
        sum_bias_down,
    )


def solution(mesh):
    vector = P(AXES)
    matrix = P(AXES, None)
    tokens = P("dp", "ctx", None)
    return jax.shard_map(
        per_device,
        mesh=mesh,
        in_specs=(
            tokens,
            P("dp"),
            vector,
            vector,
            matrix,
            vector,
            matrix,
            vector,
            vector,
            vector,
            matrix,
            vector,
            matrix,
            vector,
            tokens,
        ),
        out_specs=(
            tokens,
            tokens,
            vector,
            vector,
            matrix,
            vector,
            matrix,
            vector,
            vector,
            vector,
            matrix,
            vector,
            matrix,
            vector,
        ),
        check_vma=False,
    )
```

```python
import functools

import jax
import jax.numpy as jnp
from jax import lax
from jax.experimental import pallas as pl
from jax.experimental.pallas import tpu as pltpu
from jax.sharding import PartitionSpec as P

HEADS = 16
HD = 64
SCALE = 0.125
NEGATIVE = -1e30
AXES = ("dp", "ctx")
F32 = jnp.float32
BF16 = jnp.bfloat16


def dot_nt(a, b):
    return lax.dot_general(a, b, (((1,), (1,)), ((), ())), preferred_element_type=F32)


def dot_tn(a, b):
    return lax.dot_general(a, b, (((0,), (0,)), ((), ())), preferred_element_type=F32)


def dot_nn(a, b):
    return lax.dot_general(a, b, (((1,), (0,)), ((), ())), preferred_element_type=F32)


def allowed_keys(limit, rows, first_query, prefix_len):
    key_pos = lax.broadcasted_iota(jnp.int32, (limit, rows), 0)
    query_pos = lax.broadcasted_iota(jnp.int32, (limit, rows), 1) + first_query
    return (key_pos <= query_pos) | (key_pos < prefix_len)


def over_blocks(length, rows, step):
    if length <= 1024:
        for first in range(0, length, rows):
            step(first, max(length // 2, first + rows))
    else:

        def body(i, carry):
            step(pl.multiple_of(i * rows, rows), length)
            return carry

        lax.fori_loop(0, length // rows, body, 0)


def attend_forward(prefix_ref, q_ref, k_ref, v_ref, o_ref, lse_ref, *, rows):
    length, width = q_ref.shape
    group = width // HD
    prefix_len = prefix_ref[0]
    lane_head = lax.broadcasted_iota(jnp.int32, (1, width), 1) // HD

    def step(first, limit):
        block = pl.ds(first, rows)
        queries = q_ref[block, :] * SCALE
        keys = k_ref[:limit, :]
        values = v_ref[:limit, :]
        allowed = allowed_keys(limit, rows, first, prefix_len)
        attended = jnp.zeros((rows, width), F32)
        for h in range(group):
            mine = lane_head == h
            scores = dot_nt(keys, jnp.where(mine, queries, 0).astype(BF16))
            scores = jnp.where(allowed, scores, NEGATIVE)
            top = jnp.max(scores, axis=0, keepdims=True)
            terms = jnp.exp(scores - top)
            total = jnp.sum(terms, axis=0, keepdims=True)
            lse_ref[h, :, block] = top + jnp.log(total)
            weights = (terms * (1.0 / total)).astype(BF16)
            attended = jnp.where(mine, dot_tn(weights, values), attended)
        o_ref[block, :] = attended.astype(BF16)

    over_blocks(length, rows, step)


def attend_backward(
    prefix_ref, q_ref, k_ref, v_ref, o_ref, do_ref, lse_ref, dq_ref, dk_ref, dv_ref, dk_sum, dv_sum, *, rows
):
    length, width = q_ref.shape
    group = width // HD
    prefix_len = prefix_ref[0]
    lane_head = lax.broadcasted_iota(jnp.int32, (1, width), 1) // HD
    dk_sum[...] = jnp.zeros_like(dk_sum)
    dv_sum[...] = jnp.zeros_like(dv_sum)

    def step(first, limit):
        block = pl.ds(first, rows)
        queries = q_ref[block, :] * SCALE
        grads = do_ref[block, :]
        keys = k_ref[:limit, :]
        values = v_ref[:limit, :]
        allowed = allowed_keys(limit, rows, first, prefix_len)
        products = (grads.astype(F32) * o_ref[block, :].astype(F32)).T
        query_grad = jnp.zeros((rows, width), F32)
        for h in range(group):
            mine = lane_head == h
            queries_h = jnp.where(mine, queries, 0).astype(BF16)
            grads_h = jnp.where(mine, grads, 0).astype(BF16)
            delta = jnp.sum(products[h * HD : (h + 1) * HD, :], axis=0, keepdims=True)
            scores = jnp.where(allowed, dot_nt(keys, queries_h), NEGATIVE)
            probs = jnp.exp(scores - lse_ref[h, :, block])
            weight_grad = dot_nt(values, grads_h)
            score_grad = (probs * (weight_grad - delta)).astype(BF16)
            dv_sum[:limit, :] += dot_nn(probs.astype(BF16), grads_h)
            dk_sum[:limit, :] += dot_nn(score_grad, queries_h)
            query_grad = jnp.where(mine, dot_tn(score_grad, keys), query_grad)
        dq_ref[block, :] = (query_grad * SCALE).astype(BF16)

    over_blocks(length, rows, step)
    dk_ref[...] = dk_sum[...].astype(BF16)
    dv_ref[...] = dv_sum[...].astype(BF16)


def attention_shapes(mixed):
    length, width = mixed.shape
    heads = width // (3 * HD)
    group = 2 if heads % 2 == 0 else 1
    return length, heads, group, heads // group, group * HD


def thirds(mixed, count, lanes):
    length, width = mixed.shape
    part = lambda n: pl.BlockSpec((length, lanes), lambda g: (0, n * count + g))
    if lanes % 128 == 0:
        return [mixed] * 3, [part(0), part(1), part(2)]
    return [mixed[:, n * width // 3 : (n + 1) * width // 3] for n in range(3)], [part(0)] * 3


def attention_cost(length, heads, products):
    square = heads * length * length
    return pl.CostEstimate(
        flops=products * 4 * HD * square,
        transcendentals=square,
        bytes_accessed=2 * products * heads * length * HD * 2,
    )


def attention(prefix, mixed):
    length, heads, group, count, lanes = attention_shapes(mixed)
    operands, columns = thirds(mixed, count, lanes)
    return pl.pallas_call(
        functools.partial(attend_forward, rows=min(256, length)),
        grid=(count,),
        in_specs=[pl.BlockSpec(memory_space=pltpu.SMEM)] + columns,
        out_specs=[
            pl.BlockSpec((length, lanes), lambda g: (0, g)),
            pl.BlockSpec((group, 1, length), lambda g: (g, 0, 0)),
        ],
        out_shape=[
            jax.ShapeDtypeStruct((length, heads * HD), BF16),
            jax.ShapeDtypeStruct((heads, 1, length), F32),
        ],
        compiler_params=pltpu.CompilerParams(vmem_limit_bytes=48 * 2**20),
        cost_estimate=attention_cost(length, heads, 2),
        name="attend_forward",
    )(prefix, *operands)


def attention_grads(prefix, mixed, attended, grad_attended, log_total):
    length, heads, group, count, lanes = attention_shapes(mixed)
    operands, columns = thirds(mixed, count, lanes)
    own = pl.BlockSpec((length, lanes), lambda g: (0, g))
    wide = jax.ShapeDtypeStruct((length, heads * HD), BF16)
    return pl.pallas_call(
        functools.partial(attend_backward, rows=min(256, length)),
        grid=(count,),
        in_specs=[
            pl.BlockSpec(memory_space=pltpu.SMEM),
            *columns,
            own,
            own,
            pl.BlockSpec((group, 1, length), lambda g: (g, 0, 0)),
        ],
        out_specs=[own] * 3,
        out_shape=[wide] * 3,
        scratch_shapes=[pltpu.VMEM((length, lanes), F32)] * 2,
        compiler_params=pltpu.CompilerParams(vmem_limit_bytes=48 * 2**20),
        cost_estimate=attention_cost(length, heads, 5),
        name="attend_backward",
    )(prefix, *operands, attended, grad_attended, log_total)


def norm_project(place_ref, *refs, count):
    x_refs, refs = refs[:count], refs[count:]
    own_ref, other_ref, gain_ref, shift_ref, bias_ref, hidden_ref, mixed_ref, w_buf = refs
    tokens = x_refs[0].shape[0]
    columns = bias_ref.shape[1]
    core = place_ref[1]
    planes, rows = own_ref.shape[:2]
    for p in range(planes):
        for c, source in ((core, own_ref), (1 - core, other_ref)):
            into = pl.ds(pl.multiple_of((2 * p + c) * rows, rows), rows)
            w_buf[into, :] = source[p, :, :columns]
    for s, x_ref in enumerate(x_refs):
        values = x_ref[...].astype(F32)
        offsets = values - jnp.mean(values, axis=-1, keepdims=True)
        spread = jnp.mean(offsets * offsets, axis=-1, keepdims=True)
        hidden = offsets * lax.rsqrt(spread + 1e-05) * gain_ref[...] + shift_ref[...]
        hidden = hidden.astype(BF16)
        block = pl.ds(pl.multiple_of((place_ref[0] ^ s) * tokens, tokens), tokens)
        hidden_ref[block, :] = hidden
        mixed_ref[block, :] = (dot_nn(hidden, w_buf[...]) + bias_ref[...]).astype(BF16)


def norm_and_project(place, pieces, own, other, gain, shift, bias):
    tokens, d = pieces[0].shape
    count = len(pieces)
    vmem = pl.BlockSpec(memory_space=pltpu.VMEM)
    return pl.pallas_call(
        functools.partial(norm_project, count=count),
        in_specs=[pl.BlockSpec(memory_space=pltpu.SMEM)] + [vmem] * (count + 5),
        out_specs=[vmem, vmem],
        out_shape=[
            jax.ShapeDtypeStruct((tokens * count, d), BF16),
            jax.ShapeDtypeStruct((tokens * count, bias.shape[0]), BF16),
        ],
        scratch_shapes=[pltpu.VMEM((d, bias.shape[0]), BF16)],
        compiler_params=pltpu.CompilerParams(vmem_limit_bytes=48 * 2**20),
        name="norm_project",
    )(place, *pieces, own, other, gain[None], shift[None], bias[None])


def pack_messages(here_ref, w_ref, out_ref, *refs, sizes, width, extra):
    small, sends = refs[: len(sizes)], refs[len(sizes) :]
    count = len(sends)
    rows, d = out_ref.shape
    here = here_ref[0]
    row = lax.broadcasted_iota(jnp.int32, (rows, extra), 0)
    lane = lax.broadcasted_iota(jnp.int32, (rows, extra), 1)
    flat = row * extra + lane
    placed = jnp.zeros((rows, extra), F32)
    start = 0
    for v_ref, size in zip(small, sizes):
        spread = lax.broadcasted_iota(jnp.int32, (size, extra), 1) % size
        spread = spread == lax.broadcasted_iota(jnp.int32, (size, extra), 0)
        repeated = dot_nn(v_ref[...], jnp.where(spread, 1.0, 0.0).astype(BF16))
        first = start + here * size
        placed = jnp.where((flat >= first) & (flat < first + size), repeated, placed)
        start += size * count
    placed = placed.astype(BF16)
    for s, send_ref in enumerate(sends):
        to = here ^ s
        for part in range(3):
            columns = pl.ds(pl.multiple_of(part * d + to * width, 128), width)
            send_ref[:, part * width : (part + 1) * width] = w_ref[:, columns]
        send_ref[:, 3 * width : 3 * width + extra] = placed
        send_ref[:, 3 * width + extra :] = out_ref[...]


def first_messages(here, w_qkv, w_out, small, sizes, width, extra, count):
    rows, d = w_out.shape
    vmem = pl.BlockSpec(memory_space=pltpu.VMEM)
    return pl.pallas_call(
        functools.partial(pack_messages, sizes=sizes, width=width, extra=extra),
        in_specs=[pl.BlockSpec(memory_space=pltpu.SMEM)] + [vmem] * (2 + len(small)),
        out_specs=[vmem] * count,
        out_shape=[jax.ShapeDtypeStruct((rows, 3 * width + extra + d), BF16)] * count,
        compiler_params=pltpu.CompilerParams(vmem_limit_bytes=48 * 2**20),
        name="first_messages",
    )(here[None], w_qkv, w_out, *[v[None] for v in small])


def feed_up(x_ref, w_ref, b_ref, activ_ref, slope_ref):
    u = dot_nn(x_ref[...], w_ref[...]) + b_ref[...]
    root = 0.7978845608028654
    cube = 0.044715 * root
    square = u * u
    t = jnp.tanh(u * (root + cube * square))
    half = 0.5 + 0.5 * t
    activ = u * half
    activ_ref[...] = activ.astype(BF16)
    slope_ref[...] = half + activ * (1.0 - t) * (root + (3.0 * cube) * square)


def feed_back(cot_ref, slope_ref, down_ref, up_ref, grad_ref, sums_ref, hidden_ref):
    grad = (dot_nt(cot_ref[...], down_ref[...]) * slope_ref[...]).astype(BF16)
    grad_ref[...] = grad

    @pl.when(pl.program_id(0) == 0)
    def _():
        sums_ref[...] = jnp.zeros_like(sums_ref)

    sums_ref[...] += jnp.sum(grad.astype(F32), axis=0, keepdims=True)
    hidden_ref[...] = dot_nt(grad, up_ref[...]).astype(BF16)


def up_and_gelu(hidden, proj_up, bias):
    rows, d = hidden.shape
    units = proj_up.shape[1]
    block = min(256, rows)
    by_rows = lambda n: pl.BlockSpec((block, n), lambda i: (i, 0))
    whole = lambda m, n: pl.BlockSpec((m, n), lambda i: (0, 0))
    return pl.pallas_call(
        feed_up,
        grid=(rows // block,),
        in_specs=[by_rows(d), whole(d, units), whole(1, units)],
        out_specs=[by_rows(units), by_rows(units)],
        out_shape=[
            jax.ShapeDtypeStruct((rows, units), BF16),
            jax.ShapeDtypeStruct((rows, units), F32),
        ],
        compiler_params=pltpu.CompilerParams(vmem_limit_bytes=48 * 2**20),
        name="feed_up",
    )(hidden, proj_up, bias[None])


def hidden_grads(cot, slope, proj_down, proj_up):
    rows, units = slope.shape
    d = cot.shape[1]
    block = min(256, rows)
    by_rows = lambda n: pl.BlockSpec((block, n), lambda i: (i, 0))
    whole = lambda m, n: pl.BlockSpec((m, n), lambda i: (0, 0))
    return pl.pallas_call(
        feed_back,
        grid=(rows // block,),
        in_specs=[by_rows(d), by_rows(units), whole(units, d), whole(d, units)],
        out_specs=[by_rows(units), whole(1, units), by_rows(d)],
        out_shape=[
            jax.ShapeDtypeStruct((rows, units), BF16),
            jax.ShapeDtypeStruct((1, units), F32),
            jax.ShapeDtypeStruct((rows, d), BF16),
        ],
        compiler_params=pltpu.CompilerParams(vmem_limit_bytes=48 * 2**20),
        name="feed_back",
    )(cot, slope, proj_down, proj_up)


def bits_of(size):
    return size.bit_length() - 1


def rank(bit):
    return (0 if bit[0] == "ctx" else 1, bit[1])


def my_bit(bit):
    return (lax.axis_index(bit[0]) >> bit[1]) & 1


def swap_by(x, dp_mask, ctx_mask):
    dp, ctx = lax.axis_size("dp"), lax.axis_size("ctx")
    pairs = [
        (d * ctx + c, (d ^ dp_mask) * ctx + (c ^ ctx_mask)) for d in range(dp) for c in range(ctx)
    ]
    return lax.ppermute(x, AXES, pairs)


def swap(x, bit):
    return swap_by(x, 1 << bit[1], 0) if bit[0] == "dp" else swap_by(x, 0, 1 << bit[1])


def join(own, other, here, axis):
    first = here == 0
    return jnp.stack([jnp.where(first, own, other), jnp.where(first, other, own)], axis)


class Steps:
    def __init__(self, generator):
        self.generator = generator
        self.pending = None
        self.result = None
        self.move(None)

    def move(self, arrived):
        try:
            self.pending = self.generator.send(arrived)
        except StopIteration as stop:
            self.pending = None
            self.result = stop.value

    def finish(self):
        while self.pending is not None:
            self.move(self.pending)
        return self.result


def meet(steps, *values, held=()):
    both = [(s, True) for s in steps if s.pending is not None]
    both += [(s, False) for s in held if s.pending is not None]
    flat = [p for s, _ in both for p in s.pending]
    flat = lax.optimization_barrier((*flat, *values))
    start = 0
    for s, moves in both:
        count = len(s.pending)
        s.pending = list(flat[start : start + count])
        if moves:
            s.move(s.pending)
        start += count
    values = flat[start:]
    return values[0] if len(values) == 1 else values


def gather(x, bits, done=()):
    done = list(done)
    for bit in bits:
        place = sum(rank(d) > rank(bit) for d in done)
        (other,) = yield [swap(x, bit)]
        x = join(x, other, my_bit(bit), place)
        done.append(bit)
    return x


def scatter(x, bits, left=(), last=F32):
    remaining = sorted(list(bits) + list(left), key=rank, reverse=True)
    for n, bit in enumerate(bits):
        place = remaining.index(bit)
        here = my_bit(bit)
        sent = lax.dynamic_index_in_dim(x, 1 - here, place, keepdims=False)
        kept = lax.dynamic_index_in_dim(x, here, place, keepdims=False)
        (other,) = yield [swap(sent, bit)]
        x = kept.astype(F32) + other.astype(F32)
        remaining.pop(place)
        x = x.astype(sent.dtype if n + 1 < len(bits) else last)
    return x


def exchange(x, bits):
    remaining = sorted(bits, key=rank, reverse=True)
    done = []
    for bit in bits:
        place = remaining.index(bit)
        here = my_bit(bit)
        sent = lax.dynamic_index_in_dim(x, 1 - here, place, keepdims=False)
        kept = lax.dynamic_index_in_dim(x, here, place, keepdims=False)
        (other,) = yield [swap(sent, bit)]
        remaining.pop(place)
        place = len(remaining) + sum(rank(d) > rank(bit) for d in done)
        x = join(kept, other, here, place)
        done.append(bit)
    return x


def pool_rows(x, orders):
    count = x.shape[0] // 2
    parts = [x[:count][None], x[count:][None]]
    for bits in zip(*orders):
        others = yield [swap(part, bit) for part, bit in zip(parts, bits)]
        parts = [jnp.concatenate(both, 0) for both in zip(parts, others)]
    return jnp.concatenate(parts, 0).reshape(-1, x.shape[1])


def share_rows(x, orders):
    planes = 2 ** len(orders[0])
    x = x.reshape(2, planes, x.shape[0] // (2 * planes), x.shape[1])
    parts = [x[0], x[1]]
    for bits in zip(*(order[::-1] for order in orders)):
        count = parts[0].shape[0] // 2
        others = yield [swap(part[count:].astype(BF16), bit) for part, bit in zip(parts, bits)]
        parts = [p[:count].astype(F32) + o.astype(F32) for p, o in zip(parts, others)]
    return jnp.concatenate([p[0] for p in parts], 0)


def unrelate(pieces, me):
    for b in range(bits_of(len(pieces))):
        flip = ((me >> b) & 1) == 1
        pieces = [jnp.where(flip, pieces[j ^ (1 << b)], pieces[j]) for j in range(len(pieces))]
    return pieces


def send_others(pick):
    me = lax.axis_index("ctx")
    return [swap_by(pick(me ^ s), 0, s) for s in range(1, lax.axis_size("ctx"))]


def send_ctx(x, steps):
    ctx = lax.axis_size("ctx")
    return lax.ppermute(
        x, AXES, [(d * ctx + a, d * ctx + b) for d in range(lax.axis_size("dp")) for a, b in steps]
    )


def inner():
    z = lax.axis_index("ctx")
    return (z == 1) | (z == 2)


def ctx_bits_of():
    return [("ctx", b) for b in range(bits_of(lax.axis_size("ctx")))]


def gather_line(x):
    if lax.axis_size("ctx") != 4:
        return (yield from gather(x, ctx_bits_of()))
    pair = yield from gather(x, [("ctx", 0)])
    (middle,) = yield [send_ctx(pair, ((1, 2), (2, 1)))]
    (outer,) = yield [send_ctx(middle, ((1, 0), (2, 3)))]
    return join(pair, jnp.where(inner(), middle, outer), my_bit(("ctx", 1)), 0)


def scatter_line(x):
    if lax.axis_size("ctx") != 4:
        return (yield from scatter(x, ctx_bits_of()[::-1]))
    side = my_bit(("ctx", 1))
    far = lax.dynamic_index_in_dim(x, 1 - side, 0, keepdims=False)
    near = lax.dynamic_index_in_dim(x, side, 0, keepdims=False)
    (passed,) = yield [send_ctx(far, ((0, 1), (3, 2)))]
    far = (far.astype(F32) + passed.astype(F32)).astype(BF16)
    (crossed,) = yield [send_ctx(far, ((1, 2), (2, 1)))]
    near = (near.astype(F32) + crossed.astype(F32)).astype(BF16)
    return (yield from scatter(near, [("ctx", 0)]))


def slot_masks(bits):
    masks = [0]
    for bit in bits:
        masks += [m | 1 << bit[1] for m in masks]
    return masks


def in_pool_order(x, orders):
    planes, count, columns = x.shape
    first = slot_masks(orders[0])
    blocks = []
    for h, bits in enumerate(orders):
        for mask in slot_masks(bits):
            part = x[first.index(mask)]
            blocks.append(part[h * count // 2 : (h + 1) * count // 2])
    return jnp.concatenate(blocks, 0)


def in_chain_order(x, orders):
    planes = 2 ** len(orders[0])
    x = x.reshape(2, planes, -1, x.shape[1])
    places = [slot_masks(bits) for bits in orders]
    return jnp.stack(
        [jnp.concatenate([x[h, places[h].index(m)] for h in range(2)], 0) for m in places[0]], 0
    )


def share_chain(x, bits):
    for bit in bits[::-1]:
        count = x.shape[0] // 2
        (other,) = yield [swap(x[count:].astype(BF16), bit)]
        x = x[:count].astype(F32) + other.astype(F32)
    return x[0]


def pool_chain(x, bits):
    x = x[None]
    for bit in bits:
        (other,) = yield [swap(x, bit)]
        x = jnp.concatenate([x, other], 0)
    return x


def plane_exchange(x):
    bits = [("dp", b) for b in range(1, bits_of(lax.axis_size("dp")))]
    y = yield from exchange(x.reshape((2,) * len(bits) + x.shape[1:]), bits)
    return y.reshape(x.shape)


def core_then_line(x):
    x = yield from scatter(x, [("dp", 0)], ctx_bits_of(), BF16)
    return (yield from scatter_line(x))


def sum_planes(x):
    me = lax.axis_index("dp") >> 1
    pick = lambda p: lax.dynamic_index_in_dim(x, p, 0, keepdims=False)
    others = yield [swap_by(pick(me ^ s), s << 1, 0) for s in range(1, x.shape[0])]
    return pick(me).astype(F32) + sum(o.astype(F32) for o in others)


def other_core(x):
    (other,) = yield [swap(x, ("dp", 0))]
    return other


def pair_step(x):
    if lax.axis_size("ctx") != 4:
        return x
    return (yield from gather(x, [("ctx", 0)]))


def rest_then_core(x):
    if lax.axis_size("ctx") != 4:
        x = yield from gather(x, ctx_bits_of())
    else:
        (middle,) = yield [send_ctx(x, ((1, 2), (2, 1)))]
        (outer,) = yield [send_ctx(middle, ((1, 0), (2, 3)))]
        x = join(x, jnp.where(inner(), middle, outer), my_bit(("ctx", 1)), 0)
    (other,) = yield [swap(x, ("dp", 0))]
    return x, other


def core_line_planes(x):
    x = yield from core_then_line(x)
    return (yield from plane_exchange(x.astype(BF16)))


def normalize(values):
    center = jnp.mean(values, axis=-1, keepdims=True)
    offsets = values - center
    spread = jnp.mean(offsets * offsets, axis=-1, keepdims=True)
    scale = lax.rsqrt(spread + 1e-05)
    return offsets * scale, scale


def norm_back(grad, gain, hat, scale):
    e = grad * gain
    return scale * (
        e
        - jnp.mean(e, axis=-1, keepdims=True)
        - hat * jnp.mean(e * hat, axis=-1, keepdims=True)
    )


def gelu_tanh(values):
    return jax.nn.gelu(values, approximate=True)


def per_device(
    layer_input,
    prefix,
    ln1_gain,
    ln1_bias,
    w_qkv,
    b_qv,
    w_out,
    b_out,
    ln2_gain,
    ln2_bias,
    w_up,
    b_up,
    w_down,
    b_down,
    cotangent,
):
    dp, ctx = lax.axis_size("dp"), lax.axis_size("ctx")
    devices = dp * ctx
    planes = dp // 2
    tokens, d = layer_input.shape[1:]
    length = tokens * ctx
    width = HEADS * HD // ctx
    ff = b_up.shape[0] * devices
    units = ff // planes
    piece = b_up.shape[0]
    rows = d // devices
    core_bit = ("dp", 0)
    plane_bits = [("dp", b) for b in range(1, bits_of(dp))]
    ctx_bits = [("ctx", b) for b in range(bits_of(ctx))]
    twos = lambda bits: (2,) * len(bits)
    core = my_bit(core_bit)
    z = lax.axis_index("ctx")
    x_own = layer_input[0]
    cot_own = cotangent[0]
    orders = (plane_bits, plane_bits[::-1])
    plane = lax.axis_index("dp") >> 1

    small = [ln1_gain, ln1_bias, b_qv, b_out, ln2_gain, ln2_bias, b_up, b_down]
    sizes = [s.shape[0] for s in small]
    share = sum(sizes) * ctx
    extra = -(-share // (128 * rows)) * 128
    early = 3 * width + extra
    if all(size * ctx % extra == 0 for size in sizes) and width % 128 == 0:
        sends = first_messages(z, w_qkv, w_out, small, sizes, width, extra, ctx)
    else:
        placed = [
            jnp.where(jnp.arange(size * ctx) // size == z, jnp.tile(v, ctx), 0)
            for v, size in zip(small, sizes)
        ]
        placed = jnp.concatenate(placed + [jnp.zeros((rows * extra - share,), BF16)])
        placed = placed.reshape(rows, extra)
        by_head = w_qkv.reshape(rows, 3, ctx, width)
        sends = []
        for s in range(ctx):
            own = lax.dynamic_index_in_dim(by_head, z ^ s, 2, keepdims=False)
            sends.append(jnp.concatenate([own.reshape(rows, 3 * width), placed, w_out], 1))
    columns = [sends[0]] + [swap_by(sends[s], 0, s) for s in range(1, ctx)]
    up_rows = Steps(plane_exchange(w_up.reshape(rows, planes, units).transpose(1, 0, 2)))
    *columns, x_now, cot_now = meet([up_rows], *columns, x_own, cot_own)
    columns = jnp.stack(unrelate(columns, z), 0)

    pieces = send_others(lambda j: x_now)
    qkv = Steps(gather(columns[..., :early], plane_bits))
    pieces[0], columns, cot_now = meet([qkv, up_rows], pieces[0], columns, cot_now)
    cot = Steps(pool_chain(cot_now, plane_bits))
    out = Steps(gather(columns[..., early:], plane_bits + [core_bit]))
    feed = jnp.stack([up_rows.finish().reshape(piece, d), w_down], 0)
    feed = Steps(pair_step(feed))
    pieces[1] = meet([qkv, out, feed, cot], pieces[1])
    own = qkv.finish().reshape(planes, ctx * rows, early)
    qkv = Steps(other_core(own))
    feed = feed.finish()
    feed = feed if ctx == 4 else feed[None]
    up = Steps(rest_then_core(feed[:, 0] if ctx == 4 else feed[0, 0]))
    pieces = meet([qkv], *pieces)
    other = qkv.finish()
    lane_part = lambda t: t[..., 3 * width :].reshape(planes, ctx, rows, extra).astype(F32)
    shares = join(jnp.sum(lane_part(own), 1), jnp.sum(lane_part(other), 1), core, 1)
    shares = shares.reshape(dp, rows * extra)
    whole = []
    start = 0
    for size in sizes:
        whole.append(shares[:, start : start + size * ctx].reshape(devices * size))
        start += size * ctx
    gain_first, shift_first, bias_qv, bias_out, gain_second, shift_second, bias_up, bias_down = whole

    bias_heads = lax.dynamic_index_in_dim(bias_qv.reshape(2, ctx, width), z, 1, keepdims=False)
    bias_mixed = jnp.concatenate([bias_heads[0], jnp.zeros((width,), F32), bias_heads[1]])
    inputs_all = [x_own, *pieces]
    place = jnp.stack([z, core]).astype(jnp.int32)
    hidden_first, mixed = norm_and_project(
        place, inputs_all, own, other, gain_first, shift_first, bias_mixed
    )
    attended_heads, log_total = attention(prefix, mixed)
    attended_heads = meet([up, out], attended_heads)
    take = lambda j: lax.dynamic_slice_in_dim(attended_heads, j * tokens, tokens, 0)
    pieces = send_others(take)
    *pieces, feed = meet([], *pieces, feed, held=[cot])
    down = Steps(rest_then_core(feed[:, 1] if ctx == 4 else feed[0, 1]))
    attended = jnp.concatenate(unrelate([take(z), *pieces], z), 1)
    proj_out = out.finish().reshape(d, d)

    inputs = x_own.astype(F32)
    resid = inputs + jnp.dot(attended, proj_out, preferred_element_type=F32) + bias_out
    hat_second, scale_second = normalize(resid)
    hidden_second = (hat_second * gain_second + shift_second).astype(BF16)

    hidden = Steps(pool_rows(hidden_second, orders))
    meet([hidden, up, down])
    meet([hidden, up, down])
    across = lambda t: t.reshape(ctx, planes, rows, units).transpose(1, 0, 2, 3)
    lines, others = up.finish()
    proj_up = join(across(lines), across(others), core, 1).reshape(d, units)
    lines, others = down.finish()
    flat = lambda t: t.reshape(ctx, piece, d)
    proj_down = join(flat(lines), flat(others), core, 0).reshape(units, d)
    hidden_pool = hidden.finish()
    cot_pool = in_pool_order(cot.finish(), orders)
    bias_up_own = lax.dynamic_slice_in_dim(bias_up, plane * units, units, 0)
    activ, slope = up_and_gelu(hidden_pool, proj_up, bias_up_own)
    grad = dot_tn(activ, cot_pool).astype(BF16)
    grad, slope = meet([], grad, slope)
    down = Steps(core_then_line(grad.reshape((2,) + twos(ctx_bits) + (piece, d))))
    grad_pre, sums_pre, hidden_part = hidden_grads(cot_pool, slope, proj_down, proj_up)
    hidden_part, grad_pre = meet([], hidden_part, grad_pre)
    hidden = Steps(share_rows(hidden_part, orders))
    grad = dot_tn(hidden_pool, grad_pre).astype(BF16)
    grad = grad.reshape(planes, 2, ctx, rows, units).transpose(1, 2, 0, 3, 4)
    up = Steps(core_line_planes(grad.reshape((2,) + twos(ctx_bits) + (planes, rows, units))))
    meet([down])
    activ = meet([hidden, down], activ)
    out_part = dot_nn(activ, proj_down)
    out_part = meet([hidden, up], out_part)
    grad_hidden_second = hidden.finish()

    upstream = cot_own.astype(F32)
    grad_gain_second = jnp.sum(grad_hidden_second * hat_second, axis=0)
    grad_shift_second = jnp.sum(grad_hidden_second, axis=0)
    grad_resid = upstream + norm_back(grad_hidden_second, gain_second, hat_second, scale_second)
    grad_branch = grad_resid.astype(BF16)
    grad_bias_out = jnp.sum(grad_branch.astype(F32), axis=0)
    grad_attended = dot_nt(grad_branch, proj_out).astype(BF16)
    take = lambda j: lax.dynamic_slice_in_dim(grad_attended, j * width, width, 1)
    pieces = send_others(take)
    pieces[0] = meet([down, up], pieces[0])
    *pieces, grad_branch = meet([], *pieces, grad_branch)
    grad_heads = jnp.concatenate(unrelate([take(z), *pieces], z), 0)
    grad_q, grad_k, grad_v = attention_grads(prefix, mixed, attended_heads, grad_heads, log_total)
    grad_mixed = jnp.concatenate([grad_q, grad_k, grad_v], 1)
    wide_rows = join(own, other, core, 1)[..., : 3 * width].reshape(d, 3 * width)
    grad_hidden_all = dot_nt(grad_mixed, wide_rows)
    grad_hidden_low, grad_hidden_all, grad_mixed = meet(
        [], grad_hidden_all.astype(BF16), grad_hidden_all, grad_mixed, held=[down, up]
    )
    take = lambda j: lax.dynamic_slice_in_dim(grad_hidden_low, j * tokens, tokens, 0)
    pieces = send_others(take)
    rest = (grad_hidden_all, grad_mixed, hidden_first, attended, grad_branch, out_part)
    pieces[0], *rest, inputs_all[0] = meet([up], pieces[0], *rest, inputs_all[0], held=[down])
    grad_hidden_all, grad_mixed, hidden_first, attended, grad_branch, out_part = rest

    hat_all, _ = normalize(jnp.concatenate(unrelate(inputs_all, z), 0).astype(F32))
    sums_heads = jnp.sum(grad_mixed.astype(F32), axis=0).reshape(3, width)
    at_heads = lambda t: jnp.where(jnp.arange(d) // width == z, jnp.tile(t, ctx), 0)
    grads = [
        jnp.sum(grad_hidden_all * hat_all, axis=0),
        jnp.sum(grad_hidden_all, axis=0),
        jnp.concatenate([at_heads(sums_heads[0]), at_heads(sums_heads[2])]),
        grad_bias_out,
        grad_gain_second,
        grad_shift_second,
        jnp.where(jnp.arange(planes)[:, None] == plane, sums_pre, 0),
        jnp.sum(upstream, axis=0),
    ]
    packed = jnp.concatenate([g.reshape(dp, size * ctx) for g, size in zip(grads, sizes)], 1)
    packed = jnp.pad(packed.astype(BF16), ((0, 0), (0, rows * extra - share)))
    packed = jnp.pad(packed.reshape(dp, rows, extra), ((0, 0), (0, (ctx - 1) * rows), (0, 0)))
    grad_qkv = dot_tn(hidden_first, grad_mixed).astype(BF16).reshape(dp, ctx * rows, 3 * width)
    grad_qkv = jnp.concatenate([grad_qkv, packed], 2)
    grad_qkv = grad_qkv.reshape(twos(plane_bits) + (2, ctx * rows, early))
    qkv = Steps(scatter(grad_qkv, [core_bit] + plane_bits, (), BF16))
    grad_out = dot_tn(attended, grad_branch).astype(BF16)
    grad_out = grad_out.reshape(twos(plane_bits) + (2, ctx * rows, d))
    out = Steps(scatter(grad_out, [core_bit] + plane_bits[::-1], (), BF16))
    output = Steps(share_chain(in_chain_order(out_part, orders), plane_bits))
    meet([qkv])
    meet([out, up])
    pieces[1:] = meet([qkv, out, up, output], *pieces[1:])
    sum_down = down.finish().reshape(piece, d)
    mine = qkv.finish()
    own_small = mine[:rows, 3 * width :]
    mine = mine[:, : 3 * width].reshape(ctx, rows, 3 * width)
    mine_out = out.finish().reshape(ctx, rows, d)

    take_last = lambda j: jnp.concatenate(
        [
            lax.dynamic_index_in_dim(mine, j, 0, keepdims=False),
            own_small,
            lax.dynamic_index_in_dim(mine_out, j, 0, keepdims=False),
        ],
        1,
    )
    layer_out = (resid + output.finish() + bias_down).astype(BF16)
    terms = [take_last(z)] + send_others(take_last)
    grad_hidden_first = take(z).astype(F32) + sum(p.astype(F32) for p in pieces)
    hat_first, scale_first = normalize(inputs)
    input_grad = grad_resid + norm_back(grad_hidden_first, gain_first, hat_first, scale_first)
    columns = unrelate([t[:, : 3 * width] for t in terms], z)
    sum_qkv = jnp.stack([c.reshape(rows, 3, width) for c in columns], 2)
    sum_qkv = sum_qkv.reshape(rows, 3 * d).astype(F32)
    sum_out = sum(t[:, early:].astype(F32) for t in terms)
    packed = sum(t[:, 3 * width : early].astype(F32) for t in terms).reshape(rows * extra)
    sum_up = up.finish().astype(F32).transpose(1, 0, 2).reshape(rows, ff)
    sums = []
    start = 0
    for size in sizes:
        sums.append(lax.dynamic_slice_in_dim(packed, start + z * size, size, 0))
        start += size * ctx
    (
        sum_gain_first,
        sum_shift_first,
        sum_bias_qv,
        sum_bias_out,
        sum_gain_second,
        sum_shift_second,
        sum_bias_up,
        sum_bias_down,
    ) = sums
    return (
        layer_out[None],
        input_grad[None],
        sum_gain_first,
        sum_shift_first,
        sum_qkv,
        sum_bias_qv,
        sum_out,
        sum_bias_out,
        sum_gain_second,
        sum_shift_second,
        sum_up,
        sum_bias_up,
        sum_down,
        sum_bias_down,
    )


def solution(mesh):
    vector = P(AXES)
    matrix = P(AXES, None)
    tokens = P("dp", "ctx", None)
    return jax.shard_map(
        per_device,
        mesh=mesh,
        in_specs=(
            tokens,
            P("dp"),
            vector,
            vector,
            matrix,
            vector,
            matrix,
            vector,
            vector,
            vector,
            matrix,
            vector,
            matrix,
            vector,
            tokens,
        ),
        out_specs=(
            tokens,
            tokens,
            vector,
            vector,
            matrix,
            vector,
            matrix,
            vector,
            vector,
            vector,
            matrix,
            vector,
            matrix,
            vector,
        ),
        check_vma=False,
    )
```

```python
import functools

import jax
import jax.numpy as jnp
from jax import lax
from jax.experimental import pallas as pl
from jax.experimental.pallas import tpu as pltpu
from jax.sharding import PartitionSpec as P

HEADS = 16
HD = 64
SCALE = 0.125
NEGATIVE = -1e30
AXES = ("dp", "ctx")
F32 = jnp.float32
BF16 = jnp.bfloat16


def dot_nt(a, b):
    return lax.dot_general(a, b, (((1,), (1,)), ((), ())), preferred_element_type=F32)


def dot_tn(a, b):
    return lax.dot_general(a, b, (((0,), (0,)), ((), ())), preferred_element_type=F32)


def dot_nn(a, b):
    return lax.dot_general(a, b, (((1,), (0,)), ((), ())), preferred_element_type=F32)


def allowed_keys(limit, rows, first_query, prefix_len):
    key_pos = lax.broadcasted_iota(jnp.int32, (limit, rows), 0)
    query_pos = lax.broadcasted_iota(jnp.int32, (limit, rows), 1) + first_query
    return (key_pos <= query_pos) | (key_pos < prefix_len)


def over_blocks(length, rows, step):
    if length <= 1024:
        for first in range(0, length, rows):
            step(first, max(length // 2, first + rows))
    else:

        def body(i, carry):
            step(pl.multiple_of(i * rows, rows), length)
            return carry

        lax.fori_loop(0, length // rows, body, 0)


def attend_forward(prefix_ref, q_ref, k_ref, v_ref, o_ref, lse_ref, *, rows):
    length, width = q_ref.shape
    group = width // HD
    prefix_len = prefix_ref[0]
    lane_head = lax.broadcasted_iota(jnp.int32, (1, width), 1) // HD

    def step(first, limit):
        block = pl.ds(first, rows)
        queries = q_ref[block, :] * SCALE
        keys = k_ref[:limit, :]
        values = v_ref[:limit, :]
        allowed = allowed_keys(limit, rows, first, prefix_len)
        attended = jnp.zeros((rows, width), F32)
        for h in range(group):
            mine = lane_head == h
            scores = dot_nt(keys, jnp.where(mine, queries, 0).astype(BF16))
            scores = jnp.where(allowed, scores, NEGATIVE)
            top = jnp.max(scores, axis=0, keepdims=True)
            terms = jnp.exp(scores - top)
            total = jnp.sum(terms, axis=0, keepdims=True)
            lse_ref[h, :, block] = top + jnp.log(total)
            weights = (terms * (1.0 / total)).astype(BF16)
            attended = jnp.where(mine, dot_tn(weights, values), attended)
        o_ref[block, :] = attended.astype(BF16)

    over_blocks(length, rows, step)


def attend_backward(
    prefix_ref, q_ref, k_ref, v_ref, o_ref, do_ref, lse_ref, dq_ref, dk_ref, dv_ref, dk_sum, dv_sum, *, rows
):
    length, width = q_ref.shape
    group = width // HD
    prefix_len = prefix_ref[0]
    lane_head = lax.broadcasted_iota(jnp.int32, (1, width), 1) // HD
    dk_sum[...] = jnp.zeros_like(dk_sum)
    dv_sum[...] = jnp.zeros_like(dv_sum)

    def step(first, limit):
        block = pl.ds(first, rows)
        queries = q_ref[block, :] * SCALE
        grads = do_ref[block, :]
        keys = k_ref[:limit, :]
        values = v_ref[:limit, :]
        allowed = allowed_keys(limit, rows, first, prefix_len)
        products = (grads.astype(F32) * o_ref[block, :].astype(F32)).T
        query_grad = jnp.zeros((rows, width), F32)
        for h in range(group):
            mine = lane_head == h
            queries_h = jnp.where(mine, queries, 0).astype(BF16)
            grads_h = jnp.where(mine, grads, 0).astype(BF16)
            delta = jnp.sum(products[h * HD : (h + 1) * HD, :], axis=0, keepdims=True)
            scores = jnp.where(allowed, dot_nt(keys, queries_h), NEGATIVE)
            probs = jnp.exp(scores - lse_ref[h, :, block])
            weight_grad = dot_nt(values, grads_h)
            score_grad = (probs * (weight_grad - delta)).astype(BF16)
            dv_sum[:limit, :] += dot_nn(probs.astype(BF16), grads_h)
            dk_sum[:limit, :] += dot_nn(score_grad, queries_h)
            query_grad = jnp.where(mine, dot_tn(score_grad, keys), query_grad)
        dq_ref[block, :] = (query_grad * SCALE).astype(BF16)

    over_blocks(length, rows, step)
    dk_ref[...] = dk_sum[...].astype(BF16)
    dv_ref[...] = dv_sum[...].astype(BF16)


def attention_shapes(mixed):
    length, width = mixed.shape
    heads = width // (3 * HD)
    group = 2 if heads % 2 == 0 else 1
    return length, heads, group, heads // group, group * HD


def thirds(mixed, count, lanes):
    length, width = mixed.shape
    part = lambda n: pl.BlockSpec((length, lanes), lambda g: (0, n * count + g))
    if lanes % 128 == 0:
        return [mixed] * 3, [part(0), part(1), part(2)]
    return [mixed[:, n * width // 3 : (n + 1) * width // 3] for n in range(3)], [part(0)] * 3


def attention_cost(length, heads, products):
    square = heads * length * length
    return pl.CostEstimate(
        flops=products * 4 * HD * square,
        transcendentals=square,
        bytes_accessed=2 * products * heads * length * HD * 2,
    )


def attention(prefix, mixed):
    length, heads, group, count, lanes = attention_shapes(mixed)
    operands, columns = thirds(mixed, count, lanes)
    return pl.pallas_call(
        functools.partial(attend_forward, rows=min(256, length)),
        grid=(count,),
        in_specs=[pl.BlockSpec(memory_space=pltpu.SMEM)] + columns,
        out_specs=[
            pl.BlockSpec((length, lanes), lambda g: (0, g)),
            pl.BlockSpec((group, 1, length), lambda g: (g, 0, 0)),
        ],
        out_shape=[
            jax.ShapeDtypeStruct((length, heads * HD), BF16),
            jax.ShapeDtypeStruct((heads, 1, length), F32),
        ],
        compiler_params=pltpu.CompilerParams(vmem_limit_bytes=48 * 2**20),
        cost_estimate=attention_cost(length, heads, 2),
        name="attend_forward",
    )(prefix, *operands)


def attention_grads(prefix, mixed, attended, grad_attended, log_total):
    length, heads, group, count, lanes = attention_shapes(mixed)
    operands, columns = thirds(mixed, count, lanes)
    own = pl.BlockSpec((length, lanes), lambda g: (0, g))
    wide = jax.ShapeDtypeStruct((length, heads * HD), BF16)
    return pl.pallas_call(
        functools.partial(attend_backward, rows=min(256, length)),
        grid=(count,),
        in_specs=[
            pl.BlockSpec(memory_space=pltpu.SMEM),
            *columns,
            own,
            own,
            pl.BlockSpec((group, 1, length), lambda g: (g, 0, 0)),
        ],
        out_specs=[own] * 3,
        out_shape=[wide] * 3,
        scratch_shapes=[pltpu.VMEM((length, lanes), F32)] * 2,
        compiler_params=pltpu.CompilerParams(vmem_limit_bytes=48 * 2**20),
        cost_estimate=attention_cost(length, heads, 5),
        name="attend_backward",
    )(prefix, *operands, attended, grad_attended, log_total)


def norm_project(place_ref, *refs, count):
    x_refs, refs = refs[:count], refs[count:]
    own_ref, other_ref, gain_ref, shift_ref, bias_ref, hidden_ref, mixed_ref, w_buf = refs
    tokens = x_refs[0].shape[0]
    columns = bias_ref.shape[1]
    core = place_ref[1]
    planes, rows = own_ref.shape[:2]
    for p in range(planes):
        for c, source in ((core, own_ref), (1 - core, other_ref)):
            into = pl.ds(pl.multiple_of((2 * p + c) * rows, rows), rows)
            w_buf[into, :] = source[p, :, :columns]
    for s, x_ref in enumerate(x_refs):
        values = x_ref[...].astype(F32)
        offsets = values - jnp.mean(values, axis=-1, keepdims=True)
        spread = jnp.mean(offsets * offsets, axis=-1, keepdims=True)
        hidden = offsets * lax.rsqrt(spread + 1e-05) * gain_ref[...] + shift_ref[...]
        hidden = hidden.astype(BF16)
        block = pl.ds(pl.multiple_of((place_ref[0] ^ s) * tokens, tokens), tokens)
        hidden_ref[block, :] = hidden
        mixed_ref[block, :] = (dot_nn(hidden, w_buf[...]) + bias_ref[...]).astype(BF16)


def norm_and_project(place, pieces, own, other, gain, shift, bias):
    tokens, d = pieces[0].shape
    count = len(pieces)
    vmem = pl.BlockSpec(memory_space=pltpu.VMEM)
    return pl.pallas_call(
        functools.partial(norm_project, count=count),
        in_specs=[pl.BlockSpec(memory_space=pltpu.SMEM)] + [vmem] * (count + 5),
        out_specs=[vmem, vmem],
        out_shape=[
            jax.ShapeDtypeStruct((tokens * count, d), BF16),
            jax.ShapeDtypeStruct((tokens * count, bias.shape[0]), BF16),
        ],
        scratch_shapes=[pltpu.VMEM((d, bias.shape[0]), BF16)],
        compiler_params=pltpu.CompilerParams(vmem_limit_bytes=48 * 2**20),
        name="norm_project",
    )(place, *pieces, own, other, gain[None], shift[None], bias[None])


def pack_messages(here_ref, w_ref, out_ref, *refs, sizes, width, extra):
    small, sends = refs[: len(sizes)], refs[len(sizes) :]
    count = len(sends)
    rows, d = out_ref.shape
    here = here_ref[0]
    row = lax.broadcasted_iota(jnp.int32, (rows, extra), 0)
    lane = lax.broadcasted_iota(jnp.int32, (rows, extra), 1)
    flat = row * extra + lane
    placed = jnp.zeros((rows, extra), F32)
    start = 0
    for v_ref, size in zip(small, sizes):
        spread = lax.broadcasted_iota(jnp.int32, (size, extra), 1) % size
        spread = spread == lax.broadcasted_iota(jnp.int32, (size, extra), 0)
        repeated = dot_nn(v_ref[...], jnp.where(spread, 1.0, 0.0).astype(BF16))
        first = start + here * size
        placed = jnp.where((flat >= first) & (flat < first + size), repeated, placed)
        start += size * count
    placed = placed.astype(BF16)
    for s, send_ref in enumerate(sends):
        to = here ^ s
        for part in range(3):
            columns = pl.ds(pl.multiple_of(part * d + to * width, 128), width)
            send_ref[:, part * width : (part + 1) * width] = w_ref[:, columns]
        send_ref[:, 3 * width : 3 * width + extra] = placed
        send_ref[:, 3 * width + extra :] = out_ref[...]


def first_messages(here, w_qkv, w_out, small, sizes, width, extra, count):
    rows, d = w_out.shape
    vmem = pl.BlockSpec(memory_space=pltpu.VMEM)
    return pl.pallas_call(
        functools.partial(pack_messages, sizes=sizes, width=width, extra=extra),
        in_specs=[pl.BlockSpec(memory_space=pltpu.SMEM)] + [vmem] * (2 + len(small)),
        out_specs=[vmem] * count,
        out_shape=[jax.ShapeDtypeStruct((rows, 3 * width + extra + d), BF16)] * count,
        compiler_params=pltpu.CompilerParams(vmem_limit_bytes=48 * 2**20),
        name="first_messages",
    )(here[None], w_qkv, w_out, *[v[None] for v in small])


def feed_up(x_ref, w_ref, b_ref, activ_ref, slope_ref):
    u = dot_nn(x_ref[...], w_ref[...]) + b_ref[...]
    root = 0.7978845608028654
    cube = 0.044715 * root
    square = u * u
    t = jnp.tanh(u * (root + cube * square))
    half = 0.5 + 0.5 * t
    activ = u * half
    activ_ref[...] = activ.astype(BF16)
    slope_ref[...] = half + activ * (1.0 - t) * (root + (3.0 * cube) * square)


def feed_back(cot_ref, slope_ref, down_ref, up_ref, grad_ref, sums_ref, hidden_ref):
    grad = (dot_nt(cot_ref[...], down_ref[...]) * slope_ref[...]).astype(BF16)
    grad_ref[...] = grad

    @pl.when(pl.program_id(0) == 0)
    def _():
        sums_ref[...] = jnp.zeros_like(sums_ref)

    sums_ref[...] += jnp.sum(grad.astype(F32), axis=0, keepdims=True)
    hidden_ref[...] = dot_nt(grad, up_ref[...]).astype(BF16)


def up_and_gelu(hidden, proj_up, bias):
    rows, d = hidden.shape
    units = proj_up.shape[1]
    block = min(512, rows)
    by_rows = lambda n: pl.BlockSpec((block, n), lambda i: (i, 0))
    whole = lambda m, n: pl.BlockSpec((m, n), lambda i: (0, 0))
    return pl.pallas_call(
        feed_up,
        grid=(rows // block,),
        in_specs=[by_rows(d), whole(d, units), whole(1, units)],
        out_specs=[by_rows(units), by_rows(units)],
        out_shape=[
            jax.ShapeDtypeStruct((rows, units), BF16),
            jax.ShapeDtypeStruct((rows, units), F32),
        ],
        compiler_params=pltpu.CompilerParams(vmem_limit_bytes=48 * 2**20),
        name="feed_up",
    )(hidden, proj_up, bias[None])


def hidden_grads(cot, slope, proj_down, proj_up):
    rows, units = slope.shape
    d = cot.shape[1]
    block = min(512, rows)
    by_rows = lambda n: pl.BlockSpec((block, n), lambda i: (i, 0))
    whole = lambda m, n: pl.BlockSpec((m, n), lambda i: (0, 0))
    return pl.pallas_call(
        feed_back,
        grid=(rows // block,),
        in_specs=[by_rows(d), by_rows(units), whole(units, d), whole(d, units)],
        out_specs=[by_rows(units), whole(1, units), by_rows(d)],
        out_shape=[
            jax.ShapeDtypeStruct((rows, units), BF16),
            jax.ShapeDtypeStruct((1, units), F32),
            jax.ShapeDtypeStruct((rows, d), BF16),
        ],
        compiler_params=pltpu.CompilerParams(vmem_limit_bytes=48 * 2**20),
        name="feed_back",
    )(cot, slope, proj_down, proj_up)


def bits_of(size):
    return size.bit_length() - 1


def rank(bit):
    return (0 if bit[0] == "ctx" else 1, bit[1])


def my_bit(bit):
    return (lax.axis_index(bit[0]) >> bit[1]) & 1


def swap_by(x, dp_mask, ctx_mask):
    dp, ctx = lax.axis_size("dp"), lax.axis_size("ctx")
    pairs = [
        (d * ctx + c, (d ^ dp_mask) * ctx + (c ^ ctx_mask)) for d in range(dp) for c in range(ctx)
    ]
    return lax.ppermute(x, AXES, pairs)


def swap(x, bit):
    return swap_by(x, 1 << bit[1], 0) if bit[0] == "dp" else swap_by(x, 0, 1 << bit[1])


def join(own, other, here, axis):
    first = here == 0
    return jnp.stack([jnp.where(first, own, other), jnp.where(first, other, own)], axis)


class Steps:
    def __init__(self, generator):
        self.generator = generator
        self.pending = None
        self.result = None
        self.move(None)

    def move(self, arrived):
        try:
            self.pending = self.generator.send(arrived)
        except StopIteration as stop:
            self.pending = None
            self.result = stop.value

    def finish(self):
        while self.pending is not None:
            self.move(self.pending)
        return self.result


def meet(steps, *values, held=()):
    both = [(s, True) for s in steps if s.pending is not None]
    both += [(s, False) for s in held if s.pending is not None]
    flat = [p for s, _ in both for p in s.pending]
    flat = lax.optimization_barrier((*flat, *values))
    start = 0
    for s, moves in both:
        count = len(s.pending)
        s.pending = list(flat[start : start + count])
        if moves:
            s.move(s.pending)
        start += count
    values = flat[start:]
    return values[0] if len(values) == 1 else values


def gather(x, bits, done=()):
    done = list(done)
    for bit in bits:
        place = sum(rank(d) > rank(bit) for d in done)
        (other,) = yield [swap(x, bit)]
        x = join(x, other, my_bit(bit), place)
        done.append(bit)
    return x


def scatter(x, bits, left=(), last=F32):
    remaining = sorted(list(bits) + list(left), key=rank, reverse=True)
    for n, bit in enumerate(bits):
        place = remaining.index(bit)
        here = my_bit(bit)
        sent = lax.dynamic_index_in_dim(x, 1 - here, place, keepdims=False)
        kept = lax.dynamic_index_in_dim(x, here, place, keepdims=False)
        (other,) = yield [swap(sent, bit)]
        x = kept.astype(F32) + other.astype(F32)
        remaining.pop(place)
        x = x.astype(sent.dtype if n + 1 < len(bits) else last)
    return x


def exchange(x, bits):
    remaining = sorted(bits, key=rank, reverse=True)
    done = []
    for bit in bits:
        place = remaining.index(bit)
        here = my_bit(bit)
        sent = lax.dynamic_index_in_dim(x, 1 - here, place, keepdims=False)
        kept = lax.dynamic_index_in_dim(x, here, place, keepdims=False)
        (other,) = yield [swap(sent, bit)]
        remaining.pop(place)
        place = len(remaining) + sum(rank(d) > rank(bit) for d in done)
        x = join(kept, other, here, place)
        done.append(bit)
    return x


def pool_rows(x, orders):
    count = x.shape[0] // 2
    parts = [x[:count][None], x[count:][None]]
    for bits in zip(*orders):
        others = yield [swap(part, bit) for part, bit in zip(parts, bits)]
        parts = [jnp.concatenate(both, 0) for both in zip(parts, others)]
    return jnp.concatenate(parts, 0).reshape(-1, x.shape[1])


def share_rows(x, orders):
    planes = 2 ** len(orders[0])
    x = x.reshape(2, planes, x.shape[0] // (2 * planes), x.shape[1])
    parts = [x[0], x[1]]
    for bits in zip(*(order[::-1] for order in orders)):
        count = parts[0].shape[0] // 2
        others = yield [swap(part[count:].astype(BF16), bit) for part, bit in zip(parts, bits)]
        parts = [p[:count].astype(F32) + o.astype(F32) for p, o in zip(parts, others)]
    return jnp.concatenate([p[0] for p in parts], 0)


def unrelate(pieces, me):
    for b in range(bits_of(len(pieces))):
        flip = ((me >> b) & 1) == 1
        pieces = [jnp.where(flip, pieces[j ^ (1 << b)], pieces[j]) for j in range(len(pieces))]
    return pieces


def send_others(pick):
    me = lax.axis_index("ctx")
    return [swap_by(pick(me ^ s), 0, s) for s in range(1, lax.axis_size("ctx"))]


def send_ctx(x, steps):
    ctx = lax.axis_size("ctx")
    return lax.ppermute(
        x, AXES, [(d * ctx + a, d * ctx + b) for d in range(lax.axis_size("dp")) for a, b in steps]
    )


def inner():
    z = lax.axis_index("ctx")
    return (z == 1) | (z == 2)


def ctx_bits_of():
    return [("ctx", b) for b in range(bits_of(lax.axis_size("ctx")))]


def gather_line(x):
    if lax.axis_size("ctx") != 4:
        return (yield from gather(x, ctx_bits_of()))
    pair = yield from gather(x, [("ctx", 0)])
    (middle,) = yield [send_ctx(pair, ((1, 2), (2, 1)))]
    (outer,) = yield [send_ctx(middle, ((1, 0), (2, 3)))]
    return join(pair, jnp.where(inner(), middle, outer), my_bit(("ctx", 1)), 0)


def scatter_line(x):
    if lax.axis_size("ctx") != 4:
        return (yield from scatter(x, ctx_bits_of()[::-1]))
    side = my_bit(("ctx", 1))
    far = lax.dynamic_index_in_dim(x, 1 - side, 0, keepdims=False)
    near = lax.dynamic_index_in_dim(x, side, 0, keepdims=False)
    (passed,) = yield [send_ctx(far, ((0, 1), (3, 2)))]
    far = (far.astype(F32) + passed.astype(F32)).astype(BF16)
    (crossed,) = yield [send_ctx(far, ((1, 2), (2, 1)))]
    near = (near.astype(F32) + crossed.astype(F32)).astype(BF16)
    return (yield from scatter(near, [("ctx", 0)]))


def slot_masks(bits):
    masks = [0]
    for bit in bits:
        masks += [m | 1 << bit[1] for m in masks]
    return masks


def in_pool_order(x, orders):
    planes, count, columns = x.shape
    first = slot_masks(orders[0])
    blocks = []
    for h, bits in enumerate(orders):
        for mask in slot_masks(bits):
            part = x[first.index(mask)]
            blocks.append(part[h * count // 2 : (h + 1) * count // 2])
    return jnp.concatenate(blocks, 0)


def in_chain_order(x, orders):
    planes = 2 ** len(orders[0])
    x = x.reshape(2, planes, -1, x.shape[1])
    places = [slot_masks(bits) for bits in orders]
    return jnp.stack(
        [jnp.concatenate([x[h, places[h].index(m)] for h in range(2)], 0) for m in places[0]], 0
    )


def share_chain(x, bits):
    for bit in bits[::-1]:
        count = x.shape[0] // 2
        (other,) = yield [swap(x[count:].astype(BF16), bit)]
        x = x[:count].astype(F32) + other.astype(F32)
    return x[0]


def pool_chain(x, bits):
    x = x[None]
    for bit in bits:
        (other,) = yield [swap(x, bit)]
        x = jnp.concatenate([x, other], 0)
    return x


def plane_exchange(x):
    bits = [("dp", b) for b in range(1, bits_of(lax.axis_size("dp")))]
    y = yield from exchange(x.reshape((2,) * len(bits) + x.shape[1:]), bits)
    return y.reshape(x.shape)


def core_then_line(x):
    x = yield from scatter(x, [("dp", 0)], ctx_bits_of(), BF16)
    return (yield from scatter_line(x))


def sum_planes(x):
    me = lax.axis_index("dp") >> 1
    pick = lambda p: lax.dynamic_index_in_dim(x, p, 0, keepdims=False)
    others = yield [swap_by(pick(me ^ s), s << 1, 0) for s in range(1, x.shape[0])]
    return pick(me).astype(F32) + sum(o.astype(F32) for o in others)


def other_core(x):
    (other,) = yield [swap(x, ("dp", 0))]
    return other


def pair_step(x):
    if lax.axis_size("ctx") != 4:
        return x
    return (yield from gather(x, [("ctx", 0)]))


def rest_then_core(x):
    if lax.axis_size("ctx") != 4:
        x = yield from gather(x, ctx_bits_of())
    else:
        (middle,) = yield [send_ctx(x, ((1, 2), (2, 1)))]
        (outer,) = yield [send_ctx(middle, ((1, 0), (2, 3)))]
        x = join(x, jnp.where(inner(), middle, outer), my_bit(("ctx", 1)), 0)
    (other,) = yield [swap(x, ("dp", 0))]
    return x, other


def core_line_planes(x):
    x = yield from core_then_line(x)
    return (yield from plane_exchange(x.astype(BF16)))


def normalize(values):
    center = jnp.mean(values, axis=-1, keepdims=True)
    offsets = values - center
    spread = jnp.mean(offsets * offsets, axis=-1, keepdims=True)
    scale = lax.rsqrt(spread + 1e-05)
    return offsets * scale, scale


def norm_back(grad, gain, hat, scale):
    e = grad * gain
    return scale * (
        e
        - jnp.mean(e, axis=-1, keepdims=True)
        - hat * jnp.mean(e * hat, axis=-1, keepdims=True)
    )


def gelu_tanh(values):
    return jax.nn.gelu(values, approximate=True)


def per_device(
    layer_input,
    prefix,
    ln1_gain,
    ln1_bias,
    w_qkv,
    b_qv,
    w_out,
    b_out,
    ln2_gain,
    ln2_bias,
    w_up,
    b_up,
    w_down,
    b_down,
    cotangent,
):
    dp, ctx = lax.axis_size("dp"), lax.axis_size("ctx")
    devices = dp * ctx
    planes = dp // 2
    tokens, d = layer_input.shape[1:]
    length = tokens * ctx
    width = HEADS * HD // ctx
    ff = b_up.shape[0] * devices
    units = ff // planes
    piece = b_up.shape[0]
    rows = d // devices
    core_bit = ("dp", 0)
    plane_bits = [("dp", b) for b in range(1, bits_of(dp))]
    ctx_bits = [("ctx", b) for b in range(bits_of(ctx))]
    twos = lambda bits: (2,) * len(bits)
    core = my_bit(core_bit)
    z = lax.axis_index("ctx")
    x_own = layer_input[0]
    cot_own = cotangent[0]
    orders = (plane_bits, plane_bits[::-1])
    plane = lax.axis_index("dp") >> 1

    small = [ln1_gain, ln1_bias, b_qv, b_out, ln2_gain, ln2_bias, b_up, b_down]
    sizes = [s.shape[0] for s in small]
    share = sum(sizes) * ctx
    extra = -(-share // (128 * rows)) * 128
    early = 3 * width + extra
    if all(size * ctx % extra == extra % size == 0 for size in sizes) and width % 128 == 0:
        sends = first_messages(z, w_qkv, w_out, small, sizes, width, extra, ctx)
    else:
        placed = [
            jnp.where(jnp.arange(size * ctx) // size == z, jnp.tile(v, ctx), 0)
            for v, size in zip(small, sizes)
        ]
        placed = jnp.concatenate(placed + [jnp.zeros((rows * extra - share,), BF16)])
        placed = placed.reshape(rows, extra)
        by_head = w_qkv.reshape(rows, 3, ctx, width)
        sends = []
        for s in range(ctx):
            own = lax.dynamic_index_in_dim(by_head, z ^ s, 2, keepdims=False)
            sends.append(jnp.concatenate([own.reshape(rows, 3 * width), placed, w_out], 1))
    columns = [sends[0]] + [swap_by(sends[s], 0, s) for s in range(1, ctx)]
    up_rows = Steps(plane_exchange(w_up.reshape(rows, planes, units).transpose(1, 0, 2)))
    *columns, x_now, cot_now = meet([up_rows], *columns, x_own, cot_own)
    columns = jnp.stack(unrelate(columns, z), 0)

    pieces = send_others(lambda j: x_now)
    qkv = Steps(gather(columns[..., :early], plane_bits))
    pieces[0], columns, cot_now = meet([qkv, up_rows], pieces[0], columns, cot_now)
    cot = Steps(pool_chain(cot_now, plane_bits))
    out = Steps(gather(columns[..., early:], plane_bits + [core_bit]))
    feed = jnp.stack([up_rows.finish().reshape(piece, d), w_down], 0)
    feed = Steps(pair_step(feed))
    pieces[1] = meet([qkv, out, feed, cot], pieces[1])
    own = qkv.finish().reshape(planes, ctx * rows, early)
    qkv = Steps(other_core(own))
    feed = feed.finish()
    feed = feed if ctx == 4 else feed[None]
    up = Steps(rest_then_core(feed[:, 0] if ctx == 4 else feed[0, 0]))
    pieces = meet([qkv], *pieces)
    other = qkv.finish()
    lane_part = lambda t: t[..., 3 * width :].reshape(planes, ctx, rows, extra).astype(F32)
    shares = join(jnp.sum(lane_part(own), 1), jnp.sum(lane_part(other), 1), core, 1)
    shares = shares.reshape(dp, rows * extra)
    whole = []
    start = 0
    for size in sizes:
        whole.append(shares[:, start : start + size * ctx].reshape(devices * size))
        start += size * ctx
    gain_first, shift_first, bias_qv, bias_out, gain_second, shift_second, bias_up, bias_down = whole

    bias_heads = lax.dynamic_index_in_dim(bias_qv.reshape(2, ctx, width), z, 1, keepdims=False)
    bias_mixed = jnp.concatenate([bias_heads[0], jnp.zeros((width,), F32), bias_heads[1]])
    inputs_all = [x_own, *pieces]
    place = jnp.stack([z, core]).astype(jnp.int32)
    hidden_first, mixed = norm_and_project(
        place, inputs_all, own, other, gain_first, shift_first, bias_mixed
    )
    attended_heads, log_total = attention(prefix, mixed)
    attended_heads = meet([up, out], attended_heads)
    take = lambda j: lax.dynamic_slice_in_dim(attended_heads, j * tokens, tokens, 0)
    pieces = send_others(take)
    *pieces, feed = meet([], *pieces, feed, held=[cot])
    down = Steps(rest_then_core(feed[:, 1] if ctx == 4 else feed[0, 1]))
    attended = jnp.concatenate(unrelate([take(z), *pieces], z), 1)
    proj_out = out.finish().reshape(d, d)

    inputs = x_own.astype(F32)
    resid = inputs + jnp.dot(attended, proj_out, preferred_element_type=F32) + bias_out
    hat_second, scale_second = normalize(resid)
    hidden_second = (hat_second * gain_second + shift_second).astype(BF16)

    hidden = Steps(pool_rows(hidden_second, orders))
    meet([hidden, up, down])
    meet([hidden, up, down])
    across = lambda t: t.reshape(ctx, planes, rows, units).transpose(1, 0, 2, 3)
    lines, others = up.finish()
    proj_up = join(across(lines), across(others), core, 1).reshape(d, units)
    lines, others = down.finish()
    flat = lambda t: t.reshape(ctx, piece, d)
    proj_down = join(flat(lines), flat(others), core, 0).reshape(units, d)
    hidden_pool = hidden.finish()
    cot_pool = in_pool_order(cot.finish(), orders)
    bias_up_own = lax.dynamic_slice_in_dim(bias_up, plane * units, units, 0)
    activ, slope = up_and_gelu(hidden_pool, proj_up, bias_up_own)
    grad = dot_tn(activ, cot_pool).astype(BF16)
    grad, slope = meet([], grad, slope)
    down = Steps(core_then_line(grad.reshape((2,) + twos(ctx_bits) + (piece, d))))
    grad_pre, sums_pre, hidden_part = hidden_grads(cot_pool, slope, proj_down, proj_up)
    hidden_part, grad_pre = meet([], hidden_part, grad_pre)
    hidden = Steps(share_rows(hidden_part, orders))
    grad = dot_tn(hidden_pool, grad_pre).astype(BF16)
    grad = grad.reshape(planes, 2, ctx, rows, units).transpose(1, 2, 0, 3, 4)
    up = Steps(core_line_planes(grad.reshape((2,) + twos(ctx_bits) + (planes, rows, units))))
    meet([down])
    activ = meet([hidden, down], activ)
    out_part = dot_nn(activ, proj_down)
    out_part = meet([hidden, up], out_part)
    grad_hidden_second = hidden.finish()

    upstream = cot_own.astype(F32)
    grad_gain_second = jnp.sum(grad_hidden_second * hat_second, axis=0)
    grad_shift_second = jnp.sum(grad_hidden_second, axis=0)
    grad_resid = upstream + norm_back(grad_hidden_second, gain_second, hat_second, scale_second)
    grad_branch = grad_resid.astype(BF16)
    grad_bias_out = jnp.sum(grad_branch.astype(F32), axis=0)
    grad_attended = dot_nt(grad_branch, proj_out).astype(BF16)
    take = lambda j: lax.dynamic_slice_in_dim(grad_attended, j * width, width, 1)
    pieces = send_others(take)
    pieces[0] = meet([down, up], pieces[0])
    *pieces, grad_branch = meet([], *pieces, grad_branch)
    grad_heads = jnp.concatenate(unrelate([take(z), *pieces], z), 0)
    grad_q, grad_k, grad_v = attention_grads(prefix, mixed, attended_heads, grad_heads, log_total)
    grad_mixed = jnp.concatenate([grad_q, grad_k, grad_v], 1)
    wide_rows = join(own, other, core, 1)[..., : 3 * width].reshape(d, 3 * width)
    grad_hidden_all = dot_nt(grad_mixed, wide_rows)
    grad_hidden_low, grad_hidden_all, grad_mixed = meet(
        [], grad_hidden_all.astype(BF16), grad_hidden_all, grad_mixed, held=[down, up]
    )
    take = lambda j: lax.dynamic_slice_in_dim(grad_hidden_low, j * tokens, tokens, 0)
    pieces = send_others(take)
    rest = (grad_hidden_all, grad_mixed, hidden_first, attended, grad_branch, out_part)
    pieces[0], *rest, inputs_all[0] = meet([up], pieces[0], *rest, inputs_all[0], held=[down])
    grad_hidden_all, grad_mixed, hidden_first, attended, grad_branch, out_part = rest

    hat_all, _ = normalize(jnp.concatenate(unrelate(inputs_all, z), 0).astype(F32))
    sums_heads = jnp.sum(grad_mixed.astype(F32), axis=0).reshape(3, width)
    at_heads = lambda t: jnp.where(jnp.arange(d) // width == z, jnp.tile(t, ctx), 0)
    grads = [
        jnp.sum(grad_hidden_all * hat_all, axis=0),
        jnp.sum(grad_hidden_all, axis=0),
        jnp.concatenate([at_heads(sums_heads[0]), at_heads(sums_heads[2])]),
        grad_bias_out,
        grad_gain_second,
        grad_shift_second,
        jnp.where(jnp.arange(planes)[:, None] == plane, sums_pre, 0),
        jnp.sum(upstream, axis=0),
    ]
    packed = jnp.concatenate([g.reshape(dp, size * ctx) for g, size in zip(grads, sizes)], 1)
    packed = jnp.pad(packed.astype(BF16), ((0, 0), (0, rows * extra - share)))
    packed = jnp.pad(packed.reshape(dp, rows, extra), ((0, 0), (0, (ctx - 1) * rows), (0, 0)))
    grad_qkv = dot_tn(hidden_first, grad_mixed).astype(BF16).reshape(dp, ctx * rows, 3 * width)
    grad_qkv = jnp.concatenate([grad_qkv, packed], 2)
    grad_qkv = grad_qkv.reshape(twos(plane_bits) + (2, ctx * rows, early))
    qkv = Steps(scatter(grad_qkv, [core_bit] + plane_bits, (), BF16))
    grad_out = dot_tn(attended, grad_branch).astype(BF16)
    grad_out = grad_out.reshape(twos(plane_bits) + (2, ctx * rows, d))
    out = Steps(scatter(grad_out, [core_bit] + plane_bits[::-1], (), BF16))
    output = Steps(share_chain(in_chain_order(out_part, orders), plane_bits))
    meet([qkv])
    meet([out, up])
    pieces[1:] = meet([qkv, out, up, output], *pieces[1:])
    sum_down = down.finish().reshape(piece, d)
    mine = qkv.finish()
    own_small = mine[:rows, 3 * width :]
    mine = mine[:, : 3 * width].reshape(ctx, rows, 3 * width)
    mine_out = out.finish().reshape(ctx, rows, d)

    take_last = lambda j: jnp.concatenate(
        [
            lax.dynamic_index_in_dim(mine, j, 0, keepdims=False),
            own_small,
            lax.dynamic_index_in_dim(mine_out, j, 0, keepdims=False),
        ],
        1,
    )
    layer_out = (resid + output.finish() + bias_down).astype(BF16)
    terms = [take_last(z)] + send_others(take_last)
    grad_hidden_first = take(z).astype(F32) + sum(p.astype(F32) for p in pieces)
    hat_first, scale_first = normalize(inputs)
    input_grad = grad_resid + norm_back(grad_hidden_first, gain_first, hat_first, scale_first)
    columns = unrelate([t[:, : 3 * width] for t in terms], z)
    sum_qkv = jnp.stack([c.reshape(rows, 3, width) for c in columns], 2)
    sum_qkv = sum_qkv.reshape(rows, 3 * d).astype(F32)
    sum_out = sum(t[:, early:].astype(F32) for t in terms)
    packed = sum(t[:, 3 * width : early].astype(F32) for t in terms).reshape(rows * extra)
    sum_up = up.finish().astype(F32).transpose(1, 0, 2).reshape(rows, ff)
    sums = []
    start = 0
    for size in sizes:
        sums.append(lax.dynamic_slice_in_dim(packed, start + z * size, size, 0))
        start += size * ctx
    (
        sum_gain_first,
        sum_shift_first,
        sum_bias_qv,
        sum_bias_out,
        sum_gain_second,
        sum_shift_second,
        sum_bias_up,
        sum_bias_down,
    ) = sums
    return (
        layer_out[None],
        input_grad[None],
        sum_gain_first,
        sum_shift_first,
        sum_qkv,
        sum_bias_qv,
        sum_out,
        sum_bias_out,
        sum_gain_second,
        sum_shift_second,
        sum_up,
        sum_bias_up,
        sum_down,
        sum_bias_down,
    )


def solution(mesh):
    vector = P(AXES)
    matrix = P(AXES, None)
    tokens = P("dp", "ctx", None)
    return jax.shard_map(
        per_device,
        mesh=mesh,
        in_specs=(
            tokens,
            P("dp"),
            vector,
            vector,
            matrix,
            vector,
            matrix,
            vector,
            vector,
            vector,
            matrix,
            vector,
            matrix,
            vector,
            tokens,
        ),
        out_specs=(
            tokens,
            tokens,
            vector,
            vector,
            matrix,
            vector,
            matrix,
            vector,
            vector,
            vector,
            matrix,
            vector,
            matrix,
            vector,
        ),
        check_vma=False,
    )
```
